512 devices in a mesh: rows: 128 (over x, z, core), cols: 4 (over y).
Axes of the slice: x: 4, y: 4, z: 16, core: 2. Of those that a mesh axis runs over, the one named last changes fastest.
Arguments:
- tiles: bfloat16 [65536, 4096], P(('rows', 'cols')), may hold values from -0.125 to 0.125
- integral_cd_tile: int32 [65536], P(('rows', 'cols')), may hold values from 0 to 511
- part_dest: int32 [16384, 1], P(('rows', 'cols')), may hold values from 0 to 127; in each aligned block of 32 rows (0 to 31, 32 to 63, ...) at most 2 rows name the same one
- partial_row_place: int32 [16384], P(('rows', 'cols')), may hold values from 0 to 15
- amplitudes: bfloat16 [4, 512, 4096], P('cols', 'rows'), may hold values from -6 to 6
- residual_in: float32 [128, 16, 4096], P('rows', 'cols'), may hold values from -6 to 6
Outputs:
- residual: float32 [128, 16, 4096], P('rows', 'cols')
The draws below stay inside these ranges and needn't reach their ends.
Inputs may be any that keep to these rules, and one draw needn't show every extreme that they name: `part_dest`: among the 32 partial tiles of one device no index of rows is named more than 2 times, and at least one is named exactly 2 times.
All inputs are finite; a program needn't handle non-finite values.
Results may differ from the reference program's by a relative error of at most 0.0022.
Values may be sent and summed in bfloat16 or wider, within the bound.
A program may use at most 64 MiB of HBM per device.

```python
import math
import jax
import jax.numpy as jnp
import numpy as np
from jax import lax

TILE_SPAN = 64
NIJ = 64
TILES_PER_PART = 4
PAB = 32
OWNR = 16
INTEGRAL_HELD = 128
CD_PAIR_TILES = 512
CAP = 2
PARTIALS_PER_OUT = 8
N_ROWS = 128
N_COLS = 4


def with_ends(drawn, own_key, low, largest):
    longest = drawn.shape.index(max(drawn.shape))
    spots = []
    for shift in (0, 1):
        where = [jax.random.randint(jax.random.fold_in(own_key, axis), (), 0, length) for axis, length in enumerate(drawn.shape)]
        where[longest] = (where[longest] + shift) % drawn.shape[longest]
        spots.append(tuple(where))
    return drawn.at[spots[0]].set(low).at[spots[1]].set(largest)


def block_levels(stream_key, shape, split, least, top_value):
    level = 1.0
    for dim, shards_of in split:
        heights = jax.random.uniform(jax.random.fold_in(jax.random.fold_in(stream_key, 6), dim), (shards_of,), jnp.float32, least / len(split), top_value / len(split))
        level = level * jnp.repeat(jnp.exp(heights), shape[dim] // shards_of).reshape((-1,) + (1,) * (len(shape) - 1 - dim))
    return level


def deal_out(stream_key, own, number, rows, amount, top, reach, skew):
    sequence = jax.random.permutation(stream_key, amount)
    packed, common = load_shares(amount, rows * top, reach, skew, True), load_shares(amount, rows * top, reach, skew, False)
    places = jnp.arange(amount)

    def named(tallies, rotation):
        used = int((tallies > 0).sum())
        fixed = max(1, used // 4)
        passed = fixed + (places - fixed + rotation * (used - fixed)) % max(1, amount - fixed)
        return jnp.zeros((amount,), jnp.int32).at[sequence[jnp.where(places < fixed, places, passed)]].set(jnp.asarray(tallies, jnp.int32))

    tallies = jnp.where(number % 4 == 0, named(packed, number // 4), named(common, number - number // 4 - 1))
    mixed = jax.random.permutation(jax.random.fold_in(own, 3), amount)
    source_of, taker = mixed[0:amount // 2 * 2:2], mixed[1:amount // 2 * 2:2]
    margin = jnp.minimum(tallies[source_of] - 1, reach - tallies[taker]) // 2
    margin = jnp.where((source_of == sequence[0]) | (taker == sequence[0]) | (tallies[taker] == 0), 0, jnp.maximum(margin, 0))
    passed = jax.random.randint(jax.random.fold_in(own, 4), (amount // 2,), 0, 1 << 20) % (margin + 1)
    tallies = tallies.at[source_of].add(-passed).at[taker].add(passed)
    items = jnp.searchsorted(jnp.cumsum(tallies), jnp.arange(rows * top), side="right").astype(jnp.int32)
    grid = items.reshape(top, rows).T
    grid = grid[jax.random.permutation(jax.random.fold_in(own, 1), rows)]
    rotation = jax.random.randint(jax.random.fold_in(own, 2), (rows, 1), 0, top)
    return jnp.take_along_axis(grid, (jnp.arange(top)[None, :] + rotation) % top, axis=1)


def load_shares(amount, total, reach, skew, full):
    portions = [(1 << 20) // math.isqrt(standing ** skew) + 1 for standing in range(1, amount + 1)]
    largest = reach if full else min(reach, max(-(-total // amount), total * portions[0] // sum(portions)))
    least = 1 if total - largest >= amount - 1 else 0
    holding, surplus = [largest] + [least] * (amount - 1), total - largest - least * (amount - 1)
    while surplus > 0:
        candidates = [i for i in range(1, amount) if holding[i] < largest] or [i for i in range(1, amount) if holding[i] < reach]
        mass, budget = sum([portions[i] for i in candidates]), surplus
        for i in candidates:
            more = min(reach - holding[i], max(1, budget * portions[i] // mass), surplus)
            holding[i] = holding[i] + more
            surplus = surplus - more
    return np.array(holding)


def bell_draw(own_key, dims, spread, limit, pieces=(), kind=jnp.bfloat16):
    drawn = spread * jax.random.normal(own_key, dims, jnp.float32)
    if pieces:
        drawn = drawn * block_levels(own_key, dims, pieces, -0.22, 0.18)
    return jnp.clip(drawn, -limit, limit).astype(kind)


def setup_inputs(seed: int = 0) -> dict:
    key_of = jax.random.split(jax.random.key(seed), 7)
    tiles = bell_draw(key_of[0], (N_ROWS * N_COLS * INTEGRAL_HELD, TILE_SPAN * TILE_SPAN), (TILES_PER_PART * TILE_SPAN * PARTIALS_PER_OUT) ** -0.5, 0.125, ((0, 512),))
    integral_cd_tile = with_ends(jax.random.randint(key_of[1], (N_ROWS * N_COLS * INTEGRAL_HELD,), 0, CD_PAIR_TILES), jax.random.fold_in(key_of[1], 1), 0, CD_PAIR_TILES - 1).astype(jnp.int32)
    part_dest_keys = jax.random.split(jax.random.fold_in(key_of[2], 1), (N_ROWS * N_COLS * PAB) // PAB)
    part_dest_turns = jax.random.permutation(jax.random.fold_in(key_of[2], 3), (N_ROWS * N_COLS * PAB) // PAB)
    part_dest = jax.vmap(lambda own, number: deal_out(jax.random.fold_in(key_of[2], 2), own, number, PAB, N_ROWS, 1, CAP, 2))(part_dest_keys, part_dest_turns).reshape((N_ROWS * N_COLS * PAB, 1))
    partial_row_place = with_ends(jax.random.randint(key_of[3], (N_ROWS * N_COLS * PAB,), 0, OWNR), jax.random.fold_in(key_of[3], 1), 0, OWNR - 1).astype(jnp.int32)
    amplitudes = bell_draw(key_of[4], (N_COLS, CD_PAIR_TILES, NIJ * TILE_SPAN), 1.0, 6.0, ((0, 4), (1, 128)))
    residual_in = bell_draw(key_of[5], (N_ROWS, OWNR, NIJ * TILE_SPAN), 1.0, 6.0, ((0, 128), (1, 4)), jnp.float32)
    return dict(tiles=tiles, integral_cd_tile=integral_cd_tile, part_dest=part_dest, partial_row_place=partial_row_place, amplitudes=amplitudes, residual_in=residual_in)


def reference(tiles, integral_cd_tile, part_dest, partial_row_place, amplitudes, residual_in):
    device_count = N_ROWS * N_COLS
    flat_tiles = tiles.reshape(device_count, PAB, TILES_PER_PART, TILE_SPAN, TILE_SPAN)
    flat_cd = integral_cd_tile.reshape(device_count, PAB, TILES_PER_PART)
    target = (part_dest[:, 0] * OWNR + partial_row_place).astype(jnp.int32).reshape(device_count, PAB)

    def advance(summed, position):
        column = position % N_COLS
        panel_rows = lax.dynamic_index_in_dim(amplitudes, column, 0, keepdims=False)
        panel_rows = panel_rows.reshape(CD_PAIR_TILES, NIJ, TILE_SPAN).astype(jnp.float32)
        picked = panel_rows[flat_cd[position]]
        block_list = flat_tiles[position].astype(jnp.float32)
        partial_value = jnp.einsum('ptic,ptac->pia', picked, block_list).reshape(PAB, NIJ * TILE_SPAN)
        rounded = lax.optimization_barrier(partial_value.astype(jnp.bfloat16))
        return summed.at[target[position]].add(rounded.astype(jnp.float32)), None

    start = jnp.zeros((N_ROWS * OWNR, NIJ * TILE_SPAN), jnp.float32)
    summed, _ = lax.scan(advance, start, jnp.arange(device_count, dtype=jnp.int32))
    return residual_in + summed.reshape(N_ROWS, OWNR, NIJ * TILE_SPAN)
```

```python
import jax
import jax.numpy as jnp
from jax import lax
from jax.experimental import pallas as pl
from jax.experimental.pallas import tpu as pltpu
from jax.sharding import PartitionSpec as P

PAB = 32
HALF = 2048
MESH = pl.DeviceIdType.MESH


def coords():
    r = lax.axis_index("rows")
    y = lax.axis_index("cols")
    return r // 32, y, lax.rem(r // 2, 16), lax.rem(r, 2)


def dev(x, y, z, c):
    return ((lax.rem(x + 4, 4) * 16 + lax.rem(z + 16, 16)) * 2 + lax.rem(c, 2), lax.rem(y + 4, 4))


def ladder_kernel(
    cd_ref, codes_ref, amp_ref, tiles_ref, out_ref,
    amp, tv, tsc, wbuf, osc, xa, xb, ca, cb, sa, sb, ra, rb, se, re, sf, rf,
    tile_sem, z_s, z_r, x_s, x_r, k_s, k_r, c_s, c_r, p_s, p_r, q_s, q_r, e_s, e_r, f_s, f_r,
):
    x, y, z, c = coords()
    sent = []

    def send(src, dst, ss, rs, to):
        cp = pltpu.make_async_remote_copy(
            src_ref=src, dst_ref=dst, send_sem=ss, recv_sem=rs, device_id=to, device_id_type=MESH
        )
        cp.start()
        sent.append(cp)

    def arrived(dst, rs, to):
        pltpu.make_async_remote_copy(
            src_ref=dst, dst_ref=dst, send_sem=rs, recv_sem=rs, device_id=to, device_id_type=MESH
        ).wait_recv()

    tiles_in = pltpu.make_async_copy(tiles_ref, tv, tile_sem)
    tiles_in.start()
    sib = dev(x, y, z, c + 1)

    def spot(cc, xx, slot):
        return pl.multiple_of(((cc * 4 + xx) * 16 + slot) * 4, 4)

    def block(xx, slot, n=1, cc=None):
        return amp.at[pl.ds(spot(c if cc is None else cc, xx, slot), 4 * n)]

    amp[pl.ds(spot(c, x, 8), 4)] = amp_ref[...]
    ca[y * 2 + c] = codes_ref[...]
    cb[x * 2 + c] = codes_ref[...]

    barrier = pltpu.get_barrier_semaphore()
    friends = [dev(x, y, z + d, c) for d in (1, -1, 2, -2, 3, -3, 4, -4, 8)]
    friends += [dev(x + d, y, z, c) for d in (1, 2, 3)]
    friends += [dev(x, y + d, z, c) for d in (1, 2, 3)]
    friends += [sib]
    for t in friends:
        pl.semaphore_signal(barrier, inc=1, device_id=t, device_id_type=MESH)
    pl.semaphore_wait(barrier, len(friends))

    def z_send(slot, step):
        nslot = slot - step
        send(block(x, slot), block(x, nslot), z_s.at[nslot], z_r.at[nslot], dev(x, y, z + step, c))

    def z_wait(slot):
        arrived(block(x, slot), z_r.at[slot], sib)

    def x_send(g, slot, n):
        for i in (1, 2, 3):
            send(block(x, slot, n), block(x, slot, n), x_s.at[g, i - 1], x_r.at[g, i - 1], dev(x + i, y, z, c))

    def x_wait(g, slot, n):
        for i in (1, 2, 3):
            arrived(block(lax.rem(x + 4 - i, 4), slot, n), x_r.at[g, i - 1], sib)

    def k_send(g, slot, n):
        for i in range(4):
            xs = lax.rem(x + 4 - i, 4)
            send(block(xs, slot, n), block(xs, slot, n), k_s.at[g, i], k_r.at[g, i], sib)

    def k_wait(g, slot, n):
        for i in range(4):
            xs = lax.rem(x + 4 - i, 4)
            arrived(block(xs, slot, n, 1 - c), k_r.at[g, i], sib)

    for step in (2, -2, 1, -1):
        z_send(8, step)
    x_send(0, 8, 1)
    for i in (1, 2, 3):
        me = ca.at[y * 2 + c]
        send(me, me, c_s.at[0, i - 1], c_r.at[0, i - 1], dev(x, y + i, z, c))
        me = cb.at[x * 2 + c]
        send(me, me, c_s.at[1, i - 1], c_r.at[1, i - 1], dev(x + i, y, z, c))

    rows = lax.broadcasted_iota(jnp.int32, (128, 64), 0)
    cols = lax.broadcasted_iota(jnp.int32, (128, 64), 1)
    par = rows // 64
    ab = lax.rem(rows, 64)
    take = (cols == ab // 2 + 32 * (lax.rem(ab, 2) ^ par)).astype(jnp.bfloat16)
    keep = lax.rem(lax.broadcasted_iota(jnp.int32, (128, 512), 1), 128) // 64 == (
        lax.broadcasted_iota(jnp.int32, (128, 512), 0) // 64
    )

    def relayout(j, carry):
        base = pl.multiple_of(j * 16, 16)
        v = tv[pl.ds(base, 16), :].astype(jnp.float32)
        for l in range(32):
            tsc[pl.ds(base * 32 + l, 16, stride=32), :] = v[:, l * 128 : (l + 1) * 128]
        return carry

    def build(q, carry):
        both = []
        for t in range(4):
            b2 = tsc[pl.ds(pl.multiple_of((q * 4 + t) * 32, 32), 32), :]
            both.append(jnp.concatenate([b2, pltpu.roll(b2, 64, 1)], axis=0))
        r = jnp.concatenate(both, axis=1).astype(jnp.bfloat16)
        g = jnp.dot(take, r, preferred_element_type=jnp.float32)
        wbuf[q] = jnp.where(keep, g, 0.0).astype(jnp.bfloat16)
        return carry

    def prep(lo, hi):
        lax.fori_loop(lo // 4, hi // 4, relayout, 0)
        lax.fori_loop(lo, hi, build, 0)

    tiles_in.wait()
    prep(0, 4)
    z_wait(6)
    z_send(6, 2)
    z_send(6, 1)
    z_wait(10)
    z_send(10, -2)
    z_send(10, -1)
    z_wait(7)
    x_send(1, 6, 2)
    z_wait(9)
    x_send(2, 9, 2)
    prep(4, 8)
    z_wait(4)
    z_send(4, 2)
    z_send(4, 1)
    z_wait(12)
    z_send(12, -2)
    z_send(12, -1)
    z_wait(5)
    x_send(3, 4, 2)
    z_wait(11)
    x_send(4, 11, 2)
    prep(8, 16)
    z_wait(2)
    z_send(2, 2)
    z_send(2, 1)
    z_wait(14)
    z_send(14, -1)
    z_wait(3)
    x_send(5, 2, 2)
    z_wait(13)
    x_send(6, 13, 2)
    x_wait(0, 8, 1)
    x_wait(1, 6, 2)
    x_wait(2, 9, 2)
    x_wait(3, 4, 2)
    x_wait(4, 11, 2)
    k_send(0, 4, 9)
    for i in (1, 2, 3):
        arrived(ca.at[lax.rem(y + 4 - i, 4) * 2 + c], c_r.at[0, i - 1], sib)
        arrived(cb.at[lax.rem(x + 4 - i, 4) * 2 + c], c_r.at[1, i - 1], sib)
    for i in range(4):
        s = ca.at[lax.rem(y + 4 - i, 4) * 2 + c]
        send(s, s, c_s.at[0, 3 + i], c_r.at[0, 3 + i], sib)
        s = cb.at[lax.rem(x + 4 - i, 4) * 2 + c]
        send(s, s, c_s.at[1, 3 + i], c_r.at[1, 3 + i], sib)
    prep(16, 32)
    z_wait(0)
    z_wait(1)
    x_send(7, 0, 2)
    z_wait(15)
    x_send(8, 15, 1)
    x_wait(5, 2, 2)
    x_wait(7, 0, 2)
    k_send(1, 0, 4)
    x_wait(6, 13, 2)
    x_wait(8, 15, 1)
    k_send(2, 13, 3)
    for i in range(4):
        arrived(ca.at[lax.rem(y + 4 - i, 4) * 2 + 1 - c], c_r.at[0, 3 + i], sib)
        arrived(cb.at[lax.rem(x + 4 - i, 4) * 2 + 1 - c], c_r.at[1, 3 + i], sib)

    d = lax.broadcasted_iota(jnp.int32, (256, 256), 0)
    other = d // 64
    zz = lax.rem(d // 4, 4) * 4 + lax.rem(d // 16, 4)
    p = lax.rem(d, 4)
    lane = lax.broadcasted_iota(jnp.int32, (1, 128), 1) // 32

    def spread(ref):
        parts = []
        for h in range(2):
            row = ref[4 * h][0:1, :]
            for j in (1, 2, 3):
                row = jnp.where(lane == j, ref[4 * h + j][0:1, :], row)
            parts.append(row)
        return jnp.concatenate(parts, axis=1)

    want_a = ((other * 16 + zz) * 2 + c) * 16 + y * 4 + p
    sel_a = (spread(ca) == want_a).astype(jnp.bfloat16)
    want_b = ((x * 16 + zz) * 2 + c) * 16 + other * 4 + p
    sel_b = (spread(cb) == want_b).astype(jnp.bfloat16)

    k_wait(0, 4, 9)
    k_wait(1, 0, 4)
    k_wait(2, 13, 3)

    def product(q, carry):
        parts = []
        for t in range(4):
            cd = cd_ref[q * 4 + t]
            hr = cd // 4
            slot = lax.rem(lax.rem(hr // 2, 16) - z + 24, 16)
            parts.append(amp[((lax.rem(hr, 2) * 4 + hr // 32) * 16 + slot) * 4 + lax.rem(cd, 4)])
        a = jnp.concatenate(parts, axis=1)
        o = lax.dot_general(a, wbuf[q], (((1,), (1,)), ((), ())), preferred_element_type=jnp.float32)
        osc[pl.ds(pl.multiple_of(q * 32, 32), 32), :] = o
        return carry

    lax.fori_loop(0, PAB, product, 0)
    mine_a = xa.at[y * 2 + c]
    mine_b = xb.at[x * 2 + c]
    for r in range(16):
        mine_a[:, r * 128 : (r + 1) * 128] = osc[pl.ds(r, PAB, stride=32), :].astype(jnp.bfloat16)
    for i in (1, 2, 3):
        send(mine_a, mine_a, p_s.at[0, i - 1], p_r.at[0, i - 1], dev(x, y + i, z, c))
    for r in range(16):
        mine_b[:, r * 128 : (r + 1) * 128] = osc[pl.ds(16 + r, PAB, stride=32), :].astype(jnp.bfloat16)
    for i in (1, 2, 3):
        send(mine_b, mine_b, p_s.at[1, i - 1], p_r.at[1, i - 1], dev(x + i, y, z, c))

    for i in range(4):
        for h, (ref, me) in enumerate(((xa, y), (xb, x))):
            s = ref.at[lax.rem(me + 4 - i, 4) * 2 + c]
            if i > 0:
                arrived(s, p_r.at[h, i - 1], sib)
            send(s, s, p_s.at[h, 3 + i], p_r.at[h, 3 + i], sib)

    def dense(sel, src, dst):
        def chunk(n, carry):
            lanes = pl.ds(pl.multiple_of(n * 256, 256), 256)
            v = src[:, :, lanes].reshape(256, 256)
            s = jnp.dot(sel, v, preferred_element_type=jnp.float32).astype(jnp.bfloat16)
            dst[:, :, lanes] = s.reshape(4, 64, 256)
            return carry

        lax.fori_loop(0, HALF // 256, chunk, 0)

    for i in range(4):
        arrived(xa.at[lax.rem(y + 4 - i, 4) * 2 + 1 - c], p_r.at[0, 3 + i], sib)
    dense(sel_a, xa, sa)
    for i in (1, 2, 3):
        send(sa.at[lax.rem(x + i, 4)], ra.at[i - 1], q_s.at[0, i - 1], q_r.at[0, i - 1], dev(x + i, y, z, c))
    for i in range(4):
        arrived(xb.at[lax.rem(x + 4 - i, 4) * 2 + 1 - c], p_r.at[1, 3 + i], sib)
    dense(sel_b, xb, sb)
    for i in (1, 2, 3):
        send(sb.at[lax.rem(y + i, 4)], rb.at[i - 1], q_s.at[1, i - 1], q_r.at[1, i - 1], dev(x, y + i, z, c))

    def gathered(own, got, dst, at):
        def chunk(n, carry):
            lanes = pl.ds(pl.multiple_of(n * 256, 256), 256)
            s = own[:, lanes].astype(jnp.float32)
            for i in range(3):
                s = s + got[i, :, lanes].astype(jnp.float32)
            dst[:, :, pl.ds(pl.multiple_of(at + n * 256, 256), 256)] = s.astype(jnp.bfloat16).reshape(4, 16, 256)
            return carry

        lax.fori_loop(0, HALF // 256, chunk, 0)

    for i in (1, 2, 3):
        arrived(ra.at[i - 1], q_r.at[0, i - 1], sib)
    gathered(sa.at[x], ra, se, 0)
    for i in (1, 2, 3):
        arrived(rb.at[i - 1], q_r.at[1, i - 1], sib)
    gathered(sb.at[y], rb, se, HALF)

    a4 = z // 4
    b4 = lax.rem(z, 4)
    for i in (1, 2, 3):
        to = lax.rem(b4 + i, 4)
        send(se.at[to], re.at[i - 1], e_s.at[i - 1], e_r.at[i - 1], dev(x, y, a4 * 4 + to, c))
    for i in (1, 2, 3):
        arrived(re.at[i - 1], e_r.at[i - 1], sib)
    for u in range(4):
        lanes = slice(u * 1024, (u + 1) * 1024)
        s = se[b4, :, lanes].astype(jnp.float32)
        for i in range(3):
            s = s + re[i, :, lanes].astype(jnp.float32)
        for k in range(4):
            sf[k, u] = s[k * 4 : (k + 1) * 4, :]
    for i in (1, 2, 3):
        to = lax.rem(a4 + i, 4)
        send(sf.at[to], rf.at[i - 1], f_s.at[i - 1], f_r.at[i - 1], dev(x, y, to * 4 + b4, c))
    for i in (1, 2, 3):
        arrived(rf.at[i - 1], f_r.at[i - 1], sib)
    for u in range(4):
        out_ref[:, u * 1024 : (u + 1) * 1024] = sf[a4, u] + rf[0, u] + rf[1, u] + rf[2, u]

    for cp in sent:
        cp.wait_send()


def per_device(tiles, integral_cd_tile, part_dest, partial_row_place, amplitudes, residual_in):
    codes = jnp.tile((part_dest[:, 0] * 16 + partial_row_place)[None, :], (8, 4))
    bf16, f32, dma = jnp.bfloat16, jnp.float32, pltpu.SemaphoreType.DMA
    vmem = pl.BlockSpec(memory_space=pltpu.VMEM)
    ladder = pl.pallas_call(
        ladder_kernel,
        out_shape=jax.ShapeDtypeStruct((4, 4096), f32),
        in_specs=[
            pl.BlockSpec(memory_space=pltpu.SMEM),
            vmem,
            vmem,
            pl.BlockSpec(memory_space=pl.ANY),
        ],
        out_specs=vmem,
        scratch_shapes=[
            pltpu.VMEM((512, 32, 128), bf16),
            pltpu.VMEM((128, 4096), bf16),
            pltpu.VMEM((4096, 128), f32),
            pltpu.VMEM((32, 128, 512), bf16),
            pltpu.VMEM((1024, 128), f32),
            pltpu.VMEM((8, 32, HALF), bf16),
            pltpu.VMEM((8, 32, HALF), bf16),
            pltpu.VMEM((8, 8, 128), jnp.int32),
            pltpu.VMEM((8, 8, 128), jnp.int32),
            pltpu.VMEM((4, 64, HALF), bf16),
            pltpu.VMEM((4, 64, HALF), bf16),
            pltpu.VMEM((3, 64, HALF), bf16),
            pltpu.VMEM((3, 64, HALF), bf16),
            pltpu.VMEM((4, 16, 4096), bf16),
            pltpu.VMEM((3, 16, 4096), bf16),
            pltpu.VMEM((4, 4, 4, 1024), f32),
            pltpu.VMEM((3, 4, 4, 1024), f32),
            dma,
            dma((16,)), dma((16,)),
            dma((9, 3)), dma((9, 3)),
            dma((3, 4)), dma((3, 4)),
            dma((2, 7)), dma((2, 7)),
            dma((2, 7)), dma((2, 7)),
            dma((2, 3)), dma((2, 3)),
            dma((3,)), dma((3,)),
            dma((3,)), dma((3,)),
        ],
        compiler_params=pltpu.CompilerParams(
            collective_id=0, has_side_effects=True, vmem_limit_bytes=48 << 20
        ),
    )(integral_cd_tile, codes, amplitudes.reshape(4, 32, 128), tiles)
    return residual_in + ladder[None]


def solution(mesh):
    return jax.shard_map(
        per_device,
        mesh=mesh,
        in_specs=(
            P(("rows", "cols"), None),
            P(("rows", "cols")),
            P(("rows", "cols"), None),
            P(("rows", "cols")),
            P("cols", "rows", None),
            P("rows", "cols", None),
        ),
        out_specs=P("rows", "cols", None),
        check_vma=False,
    )
```

```python
import jax
import jax.numpy as jnp
from jax import lax
from jax.experimental import pallas as pl
from jax.experimental.pallas import tpu as pltpu
from jax.sharding import PartitionSpec as P

PAB = 32
HALF = 2048
MESH = pl.DeviceIdType.MESH


def coords():
    r = lax.axis_index("rows")
    y = lax.axis_index("cols")
    return r // 32, y, lax.rem(r // 2, 16), lax.rem(r, 2)


def dev(x, y, z, c):
    return ((lax.rem(x + 4, 4) * 16 + lax.rem(z + 16, 16)) * 2 + lax.rem(c, 2), lax.rem(y + 4, 4))


def ladder_kernel(
    cd_hbm, dest_hbm, place_hbm, amp_hbm, tiles_hbm, out_ref,
    cd_ref, dest, place, amp4, amp, tv, tsc, wbuf, osc, xa, xb, ca, cb, sa, sb, ra, rb, se, re, sf, rf,
    in_sem, z_s, z_r, x_s, x_r, k_s, k_r, c_s, c_r, p_s, p_r, q_s, q_r, e_s, e_r, f_s, f_r,
):
    x, y, z, c = coords()
    sent = []

    def send(src, dst, ss, rs, to):
        cp = pltpu.make_async_remote_copy(
            src_ref=src, dst_ref=dst, send_sem=ss, recv_sem=rs, device_id=to, device_id_type=MESH
        )
        cp.start()
        sent.append(cp)

    def arrived(dst, rs, to):
        pltpu.make_async_remote_copy(
            src_ref=dst, dst_ref=dst, send_sem=rs, recv_sem=rs, device_id=to, device_id_type=MESH
        ).wait_recv()

    sib = dev(x, y, z, c + 1)
    barrier = pltpu.get_barrier_semaphore()
    friends = [dev(x, y, z + d, c) for d in (1, -1, 2, -2, 4, -4, 8)]
    friends += [dev(x + d, y, z, c) for d in (1, 2, 3)]
    friends += [dev(x, y + d, z, c) for d in (1, 2, 3)]
    friends += [sib]
    for t in friends:
        pl.semaphore_signal(barrier, inc=1, device_id=t, device_id_type=MESH)
    loads = []
    for i, (src, dst) in enumerate(
        ((amp_hbm, amp4), (dest_hbm, dest), (place_hbm, place), (cd_hbm, cd_ref), (tiles_hbm, tv))
    ):
        loads.append(pltpu.make_async_copy(src, dst, in_sem.at[i]))
        loads[-1].start()

    def spot(cc, xx, slot):
        return pl.multiple_of(((cc * 4 + xx) * 16 + slot) * 4, 4)

    def block(xx, slot, n=1, cc=None):
        return amp.at[pl.ds(spot(c if cc is None else cc, xx, slot), 4 * n)]

    for i in range(3):
        loads[i].wait()
    v = amp4[...].astype(jnp.float32)
    for l in range(32):
        osc[pl.ds(l, 4, stride=32), :] = v[:, l * 128 : (l + 1) * 128]
    amp[pl.ds(spot(c, x, 8), 4)] = osc[0:128, :].reshape(4, 32, 128).astype(jnp.bfloat16)
    code = dest[...] * 16 + place[...]
    code = jnp.broadcast_to(jnp.concatenate([code] * 4, axis=1), (8, 128))
    ca[y * 2 + c] = code
    cb[x * 2 + c] = code
    pl.semaphore_wait(barrier, len(friends))

    def z_send(slot, step):
        nslot = slot - step
        send(block(x, slot), block(x, nslot), z_s.at[nslot], z_r.at[nslot], dev(x, y, z + step, c))

    def z_wait(slot):
        arrived(block(x, slot), z_r.at[slot], sib)

    def x_send(g, slot, n):
        for i in (1, 2, 3):
            send(block(x, slot, n), block(x, slot, n), x_s.at[g, i - 1], x_r.at[g, i - 1], dev(x + i, y, z, c))

    def x_wait(g, slot, n):
        for i in (1, 2, 3):
            arrived(block(lax.rem(x + 4 - i, 4), slot, n), x_r.at[g, i - 1], sib)

    def k_send(g, slot, n):
        for i in range(4):
            xs = lax.rem(x + 4 - i, 4)
            send(block(xs, slot, n), block(xs, slot, n), k_s.at[g, i], k_r.at[g, i], sib)

    def k_wait(g, slot, n):
        for i in range(4):
            xs = lax.rem(x + 4 - i, 4)
            arrived(block(xs, slot, n, 1 - c), k_r.at[g, i], sib)

    for step in (2, -2, 1, -1):
        z_send(8, step)
    x_send(0, 8, 1)
    for i in (1, 2, 3):
        me = ca.at[y * 2 + c]
        send(me, me, c_s.at[0, i - 1], c_r.at[0, i - 1], dev(x, y + i, z, c))
        me = cb.at[x * 2 + c]
        send(me, me, c_s.at[1, i - 1], c_r.at[1, i - 1], dev(x + i, y, z, c))

    rows = lax.broadcasted_iota(jnp.int32, (128, 64), 0)
    cols = lax.broadcasted_iota(jnp.int32, (128, 64), 1)
    par = rows // 64
    ab = lax.rem(rows, 64)
    take = (cols == ab // 2 + 32 * (lax.rem(ab, 2) ^ par)).astype(jnp.bfloat16)
    keep = lax.rem(lax.broadcasted_iota(jnp.int32, (128, 512), 1), 128) // 64 == (
        lax.broadcasted_iota(jnp.int32, (128, 512), 0) // 64
    )

    def relayout(j, carry):
        base = pl.multiple_of(j * 16, 16)
        v = tv[pl.ds(base, 16), :].astype(jnp.float32)
        for l in range(32):
            tsc[pl.ds(base * 32 + l, 16, stride=32), :] = v[:, l * 128 : (l + 1) * 128]
        return carry

    def build(q, carry):
        both = []
        for t in range(4):
            b2 = tsc[pl.ds(pl.multiple_of((q * 4 + t) * 32, 32), 32), :]
            both.append(jnp.concatenate([b2, pltpu.roll(b2, 64, 1)], axis=0))
        r = jnp.concatenate(both, axis=1).astype(jnp.bfloat16)
        g = jnp.dot(take, r, preferred_element_type=jnp.float32)
        wbuf[q] = jnp.where(keep, g, 0.0).astype(jnp.bfloat16)
        return carry

    def prep(lo, hi):
        lax.fori_loop(lo // 4, hi // 4, relayout, 0)
        lax.fori_loop(lo, hi, build, 0)

    loads[3].wait()
    loads[4].wait()
    prep(0, 4)
    z_wait(6)
    z_send(6, 2)
    z_send(6, 1)
    z_wait(10)
    z_send(10, -2)
    z_send(10, -1)
    z_wait(7)
    x_send(1, 6, 2)
    z_wait(9)
    x_send(2, 9, 2)
    prep(4, 8)
    z_wait(4)
    z_send(4, 2)
    z_send(4, 1)
    z_wait(12)
    z_send(12, -2)
    z_send(12, -1)
    z_wait(5)
    x_send(3, 4, 2)
    z_wait(11)
    x_send(4, 11, 2)
    prep(8, 16)
    z_wait(2)
    z_send(2, 2)
    z_send(2, 1)
    z_wait(14)
    z_send(14, -1)
    z_wait(3)
    x_send(5, 2, 2)
    z_wait(13)
    x_send(6, 13, 2)
    x_wait(0, 8, 1)
    x_wait(1, 6, 2)
    x_wait(2, 9, 2)
    x_wait(3, 4, 2)
    x_wait(4, 11, 2)
    k_send(0, 4, 9)
    for i in (1, 2, 3):
        arrived(ca.at[lax.rem(y + 4 - i, 4) * 2 + c], c_r.at[0, i - 1], sib)
        arrived(cb.at[lax.rem(x + 4 - i, 4) * 2 + c], c_r.at[1, i - 1], sib)
    for i in range(4):
        s = ca.at[lax.rem(y + 4 - i, 4) * 2 + c]
        send(s, s, c_s.at[0, 3 + i], c_r.at[0, 3 + i], sib)
        s = cb.at[lax.rem(x + 4 - i, 4) * 2 + c]
        send(s, s, c_s.at[1, 3 + i], c_r.at[1, 3 + i], sib)
    prep(16, 32)
    z_wait(0)
    z_wait(1)
    x_send(7, 0, 2)
    z_wait(15)
    x_send(8, 15, 1)
    x_wait(5, 2, 2)
    k_send(1, 2, 2)
    x_wait(6, 13, 2)
    k_send(2, 13, 2)
    x_wait(7, 0, 2)
    k_send(3, 0, 2)
    x_wait(8, 15, 1)
    k_send(4, 15, 1)
    for i in range(4):
        arrived(ca.at[lax.rem(y + 4 - i, 4) * 2 + 1 - c], c_r.at[0, 3 + i], sib)
        arrived(cb.at[lax.rem(x + 4 - i, 4) * 2 + 1 - c], c_r.at[1, 3 + i], sib)

    d = lax.broadcasted_iota(jnp.int32, (256, 256), 0)
    other = d // 64
    zz = lax.rem(d // 4, 4) * 4 + lax.rem(d // 16, 4)
    p = lax.rem(d, 4)
    lane = lax.broadcasted_iota(jnp.int32, (1, 128), 1) // 32

    def spread(ref):
        parts = []
        for h in range(2):
            row = ref[4 * h][0:1, :]
            for j in (1, 2, 3):
                row = jnp.where(lane == j, ref[4 * h + j][0:1, :], row)
            parts.append(row)
        return jnp.concatenate(parts, axis=1)

    want_a = ((other * 16 + zz) * 2 + c) * 16 + y * 4 + p
    sel_a = (spread(ca) == want_a).astype(jnp.bfloat16)
    want_b = ((x * 16 + zz) * 2 + c) * 16 + other * 4 + p
    sel_b = (spread(cb) == want_b).astype(jnp.bfloat16)

    k_wait(0, 4, 9)
    k_wait(1, 2, 2)
    k_wait(2, 13, 2)
    k_wait(3, 0, 2)
    k_wait(4, 15, 1)

    def product(q, carry):
        parts = []
        for t in range(4):
            cd = cd_ref[q * 4 + t]
            hr = cd // 4
            slot = lax.rem(lax.rem(hr // 2, 16) - z + 24, 16)
            parts.append(amp[((lax.rem(hr, 2) * 4 + hr // 32) * 16 + slot) * 4 + lax.rem(cd, 4)])
        a = jnp.concatenate(parts, axis=1)
        o = lax.dot_general(a, wbuf[q], (((1,), (1,)), ((), ())), preferred_element_type=jnp.float32)
        osc[pl.ds(pl.multiple_of(q * 32, 32), 32), :] = o
        return carry

    def mine(h, j):
        ref, me = ((xa, y), (xb, x))[h]
        return lambda i: ref.at[lax.rem(me + 4 - i, 4) * 2 + c, pl.ds(j * 16, 16), :]

    def theirs(h, j, i):
        ref, me = ((xa, y), (xb, x))[h]
        return ref.at[lax.rem(me + 4 - i, 4) * 2 + 1 - c, pl.ds(j * 16, 16), :]

    for j in range(2):
        lax.fori_loop(j * 16, j * 16 + 16, product, 0)
        for h in range(2):
            own = mine(h, j)(0)
            for r in range(16):
                v = osc[pl.ds(j * 512 + h * 16 + r, 16, stride=32), :]
                own[:, r * 128 : (r + 1) * 128] = v.astype(jnp.bfloat16)
            for i in (1, 2, 3):
                to = dev(x, y + i, z, c) if h == 0 else dev(x + i, y, z, c)
                send(own, own, p_s.at[h, j, i - 1], p_r.at[h, j, i - 1], to)
            send(own, own, p_s.at[h, j, 3], p_r.at[h, j, 3], sib)
    for h in range(2):
        for j in range(2):
            for i in (1, 2, 3):
                got = mine(h, j)(i)
                arrived(got, p_r.at[h, j, i - 1], sib)
                send(got, got, p_s.at[h, j, 3 + i], p_r.at[h, j, 3 + i], sib)

    def dense(sel, src, dst):
        def chunk(n, carry):
            lanes = pl.ds(pl.multiple_of(n * 256, 256), 256)
            v = src[:, :, lanes].reshape(256, 256)
            s = jnp.dot(sel, v, preferred_element_type=jnp.float32).astype(jnp.bfloat16)
            dst[:, :, lanes] = s.reshape(4, 64, 256)
            return carry

        lax.fori_loop(0, HALF // 256, chunk, 0)

    def exchange(h, sel, src, dst, got):
        for j in range(2):
            for i in range(4):
                arrived(theirs(h, j, i), p_r.at[h, j, 3 + i], sib)
        dense(sel, src, dst)
        for i in (1, 2, 3):
            to = dev(x + i, y, z, c) if h == 0 else dev(x, y + i, z, c)
            me = x if h == 0 else y
            send(dst.at[lax.rem(me + i, 4)], got.at[i - 1], q_s.at[h, i - 1], q_r.at[h, i - 1], to)

    exchange(0, sel_a, xa, sa, ra)
    exchange(1, sel_b, xb, sb, rb)

    b4 = lax.rem(z, 4)
    a4 = z // 4

    def gathered(h, own, got):
        for i in (1, 2, 3):
            arrived(got.at[i - 1], q_r.at[h, i - 1], sib)

        def chunk(n, carry):
            lanes = pl.ds(pl.multiple_of(n * 256, 256), 256)
            s = own[:, lanes].astype(jnp.float32)
            for i in range(3):
                s = s + got[i, :, lanes].astype(jnp.float32)
            se[h, :, :, lanes] = s.astype(jnp.bfloat16).reshape(4, 16, 256)
            return carry

        lax.fori_loop(0, HALF // 256, chunk, 0)
        for i, step in enumerate((1, -1, 2 * (2 * h - 1))):
            to = lax.rem(b4 + step + 4, 4)
            send(se.at[h, to], re.at[h, i], e_s.at[h, i], e_r.at[h, i], dev(x, y, z + step, c))

    def fours(h):
        for i in range(3):
            arrived(re.at[h, i], e_r.at[h, i], sib)
        parts = []
        for u in range(4):
            lanes = slice(u * 512, (u + 1) * 512)
            s = se[h, b4, :, lanes].astype(jnp.float32)
            for i in range(3):
                s = s + re[h, i, :, lanes].astype(jnp.float32)
            parts.append(s)
        for k in range(4):
            v = jnp.concatenate([s[k * 4 : (k + 1) * 4, :] for s in parts], axis=0)
            sf[h, k] = v.astype(jnp.bfloat16)
        for i in (1, 2, 3):
            to = lax.rem(a4 + i, 4)
            send(sf.at[h, to], rf.at[h, i - 1], f_s.at[h, i - 1], f_r.at[h, i - 1], dev(x, y, z + 4 * i, c))

    def finish(h):
        s = sf[h, a4].astype(jnp.float32)
        for i in range(3):
            arrived(rf.at[h, i], f_r.at[h, i], sib)
            s = s + rf[h, i].astype(jnp.float32)
        for u in range(4):
            at = h * HALF + u * 512
            out_ref[:, at : at + 512] = s[u * 4 : (u + 1) * 4, :]

    gathered(0, sa.at[x], ra)
    gathered(1, sb.at[y], rb)
    fours(0)
    fours(1)
    finish(0)
    finish(1)

    for cp in sent:
        cp.wait_send()


def per_device(tiles, integral_cd_tile, part_dest, partial_row_place, amplitudes, residual_in):
    bf16, f32, i32, dma = jnp.bfloat16, jnp.float32, jnp.int32, pltpu.SemaphoreType.DMA
    hbm = pl.BlockSpec(memory_space=pltpu.HBM)
    ladder = pl.pallas_call(
        ladder_kernel,
        out_shape=jax.ShapeDtypeStruct((4, 4096), f32),
        in_specs=[hbm] * 5,
        out_specs=pl.BlockSpec(memory_space=pltpu.VMEM),
        scratch_shapes=[
            pltpu.SMEM((128,), i32),
            pltpu.VMEM((1, 32), i32),
            pltpu.VMEM((1, 32), i32),
            pltpu.VMEM((4, 4096), bf16),
            pltpu.VMEM((512, 32, 128), bf16),
            pltpu.VMEM((128, 4096), bf16),
            pltpu.VMEM((4096, 128), f32),
            pltpu.VMEM((32, 128, 512), bf16),
            pltpu.VMEM((1024, 128), f32),
            pltpu.VMEM((8, 32, HALF), bf16),
            pltpu.VMEM((8, 32, HALF), bf16),
            pltpu.VMEM((8, 8, 128), i32),
            pltpu.VMEM((8, 8, 128), i32),
            pltpu.VMEM((4, 64, HALF), bf16),
            pltpu.VMEM((4, 64, HALF), bf16),
            pltpu.VMEM((3, 64, HALF), bf16),
            pltpu.VMEM((3, 64, HALF), bf16),
            pltpu.VMEM((2, 4, 16, HALF), bf16),
            pltpu.VMEM((2, 3, 16, HALF), bf16),
            pltpu.VMEM((2, 4, 16, 512), bf16),
            pltpu.VMEM((2, 3, 16, 512), bf16),
            dma((5,)),
            dma((16,)), dma((16,)),
            dma((9, 3)), dma((9, 3)),
            dma((5, 4)), dma((5, 4)),
            dma((2, 7)), dma((2, 7)),
            dma((2, 2, 7)), dma((2, 2, 7)),
            dma((2, 3)), dma((2, 3)),
            dma((2, 3)), dma((2, 3)),
            dma((2, 3)), dma((2, 3)),
        ],
        compiler_params=pltpu.CompilerParams(
            collective_id=0, has_side_effects=True, vmem_limit_bytes=63 << 20
        ),
    )(
        integral_cd_tile,
        part_dest.reshape(1, PAB),
        partial_row_place.reshape(1, PAB),
        amplitudes.reshape(4, 4096),
        tiles,
    )
    return residual_in + ladder[None]


def solution(mesh):
    return jax.shard_map(
        per_device,
        mesh=mesh,
        in_specs=(
            P(("rows", "cols"), None),
            P(("rows", "cols")),
            P(("rows", "cols"), None),
            P(("rows", "cols")),
            P("cols", "rows", None),
            P("rows", "cols", None),
        ),
        out_specs=P("rows", "cols", None),
        check_vma=False,
    )
```

```python
import jax
import jax.numpy as jnp
from jax import lax
from jax.experimental import pallas as pl
from jax.experimental.pallas import tpu as pltpu
from jax.sharding import PartitionSpec as P

PAB = 32
HALF = 2048
LANES = 1024
MESH = pl.DeviceIdType.MESH


def coords():
    r = lax.axis_index("rows")
    y = lax.axis_index("cols")
    return r // 32, y, lax.rem(r // 2, 16), lax.rem(r, 2)


def dev(x, y, z, c):
    return ((lax.rem(x + 4, 4) * 16 + lax.rem(z + 16, 16)) * 2 + lax.rem(c, 2), lax.rem(y + 4, 4))


def ladder_kernel(
    cd_hbm, dest_hbm, place_hbm, amp_hbm, tiles_hbm, out_ref,
    cd_ref, dest, place, amp4, amp, tv, tsc, wbuf, osc, xa, xb, ca, cb, sd, rd, se, re, sf, rf,
    in_sem, z_s, z_r, x_s, x_r, k_s, k_r, c_s, c_r, p_s, p_r, q_s, q_r, e_s, e_r, f_s, f_r,
):
    x, y, z, c = coords()
    sent = []

    def send(src, dst, ss, rs, to):
        cp = pltpu.make_async_remote_copy(
            src_ref=src, dst_ref=dst, send_sem=ss, recv_sem=rs, device_id=to, device_id_type=MESH
        )
        cp.start()
        sent.append(cp)

    def arrived(dst, rs, to):
        pltpu.make_async_remote_copy(
            src_ref=dst, dst_ref=dst, send_sem=rs, recv_sem=rs, device_id=to, device_id_type=MESH
        ).wait_recv()

    sib = dev(x, y, z, c + 1)
    barrier = pltpu.get_barrier_semaphore()
    friends = [dev(x, y, z + d, c) for d in (1, -1, 2, -2)]
    friends += [dev(x + d, y, z, c) for d in (1, 2, 3)]
    friends += [dev(x, y + d, z, c) for d in (1, 2, 3)]
    friends += [sib]
    for t in friends:
        pl.semaphore_signal(barrier, inc=1, device_id=t, device_id_type=MESH)
    loads = []
    for i, (src, dst) in enumerate(
        ((amp_hbm, amp4), (dest_hbm, dest), (place_hbm, place), (cd_hbm, cd_ref), (tiles_hbm, tv))
    ):
        loads.append(pltpu.make_async_copy(src, dst, in_sem.at[i]))
        loads[-1].start()

    def spot(cc, xx, slot):
        return pl.multiple_of(((cc * 4 + xx) * 16 + slot) * 4, 4)

    def block(xx, slot, n=1, cc=None):
        return amp.at[pl.ds(spot(c if cc is None else cc, xx, slot), 4 * n)]

    for i in range(3):
        loads[i].wait()
    v = amp4[...].astype(jnp.float32)
    for l in range(32):
        osc[pl.ds(l, 4, stride=32), :] = v[:, l * 128 : (l + 1) * 128]
    amp[pl.ds(spot(c, x, 8), 4)] = osc[0:128, :].reshape(4, 32, 128).astype(jnp.bfloat16)
    code = dest[...] * 16 + place[...]
    code = jnp.broadcast_to(jnp.concatenate([code] * 4, axis=1), (8, 128))
    ca[y * 2 + c] = code
    cb[x * 2 + c] = code
    pl.semaphore_wait(barrier, len(friends))

    def z_send(slot, step):
        nslot = slot - step
        send(block(x, slot), block(x, nslot), z_s.at[nslot], z_r.at[nslot], dev(x, y, z + step, c))

    def z_wait(slot):
        arrived(block(x, slot), z_r.at[slot], sib)

    def x_send(g, slot, n):
        for i in (1, 2, 3):
            send(block(x, slot, n), block(x, slot, n), x_s.at[g, i - 1], x_r.at[g, i - 1], dev(x + i, y, z, c))

    def x_wait(g, slot, n):
        for i in (1, 2, 3):
            arrived(block(lax.rem(x + 4 - i, 4), slot, n), x_r.at[g, i - 1], sib)

    def k_send(g, slot, n):
        for i in range(4):
            xs = lax.rem(x + 4 - i, 4)
            send(block(xs, slot, n), block(xs, slot, n), k_s.at[g, i], k_r.at[g, i], sib)

    def k_wait(g, slot, n):
        for i in range(4):
            xs = lax.rem(x + 4 - i, 4)
            arrived(block(xs, slot, n, 1 - c), k_r.at[g, i], sib)

    for step in (2, -2, 1, -1):
        z_send(8, step)
    x_send(0, 8, 1)
    for i in (1, 2, 3):
        me = ca.at[y * 2 + c]
        send(me, me, c_s.at[0, i - 1], c_r.at[0, i - 1], dev(x, y + i, z, c))
        me = cb.at[x * 2 + c]
        send(me, me, c_s.at[1, i - 1], c_r.at[1, i - 1], dev(x + i, y, z, c))

    rows = lax.broadcasted_iota(jnp.int32, (128, 64), 0)
    cols = lax.broadcasted_iota(jnp.int32, (128, 64), 1)
    par = rows // 64
    ab = lax.rem(rows, 64)
    take = (cols == ab // 2 + 32 * (lax.rem(ab, 2) ^ par)).astype(jnp.bfloat16)
    keep = lax.rem(lax.broadcasted_iota(jnp.int32, (128, 512), 1), 128) // 64 == (
        lax.broadcasted_iota(jnp.int32, (128, 512), 0) // 64
    )

    def relayout(j, carry):
        base = pl.multiple_of(j * 16, 16)
        v = tv[pl.ds(base, 16), :].astype(jnp.float32)
        for l in range(32):
            tsc[pl.ds(base * 32 + l, 16, stride=32), :] = v[:, l * 128 : (l + 1) * 128]
        return carry

    def build(q, carry):
        both = []
        for t in range(4):
            b2 = tsc[pl.ds(pl.multiple_of((q * 4 + t) * 32, 32), 32), :]
            both.append(jnp.concatenate([b2, pltpu.roll(b2, 64, 1)], axis=0))
        r = jnp.concatenate(both, axis=1).astype(jnp.bfloat16)
        g = jnp.dot(take, r, preferred_element_type=jnp.float32)
        wbuf[q] = jnp.where(keep, g, 0.0).astype(jnp.bfloat16)
        return carry

    def prep(lo, hi):
        lax.fori_loop(lo // 4, hi // 4, relayout, 0)
        lax.fori_loop(lo, hi, build, 0)

    loads[3].wait()
    loads[4].wait()
    prep(0, 4)
    z_wait(6)
    z_send(6, 2)
    z_send(6, 1)
    z_wait(10)
    z_send(10, -2)
    z_send(10, -1)
    z_wait(7)
    x_send(1, 6, 2)
    z_wait(9)
    x_send(2, 9, 2)
    prep(4, 8)
    z_wait(4)
    z_send(4, 2)
    z_send(4, 1)
    z_wait(12)
    z_send(12, -2)
    z_send(12, -1)
    z_wait(5)
    x_send(3, 4, 2)
    z_wait(11)
    x_send(4, 11, 2)
    prep(8, 16)
    z_wait(2)
    z_send(2, 2)
    z_send(2, 1)
    z_wait(14)
    z_send(14, -1)
    z_wait(3)
    x_send(5, 2, 2)
    z_wait(13)
    x_send(6, 13, 2)
    x_wait(0, 8, 1)
    x_wait(1, 6, 2)
    x_wait(2, 9, 2)
    x_wait(3, 4, 2)
    x_wait(4, 11, 2)
    k_send(0, 4, 9)
    for i in (1, 2, 3):
        arrived(ca.at[lax.rem(y + 4 - i, 4) * 2 + c], c_r.at[0, i - 1], sib)
        arrived(cb.at[lax.rem(x + 4 - i, 4) * 2 + c], c_r.at[1, i - 1], sib)
    for i in range(4):
        s = ca.at[lax.rem(y + 4 - i, 4) * 2 + c]
        send(s, s, c_s.at[0, 3 + i], c_r.at[0, 3 + i], sib)
        s = cb.at[lax.rem(x + 4 - i, 4) * 2 + c]
        send(s, s, c_s.at[1, 3 + i], c_r.at[1, 3 + i], sib)
    prep(16, 32)
    z_wait(0)
    z_wait(1)
    x_send(7, 0, 2)
    z_wait(15)
    x_send(8, 15, 1)
    x_wait(5, 2, 2)
    k_send(1, 2, 2)
    x_wait(6, 13, 2)
    k_send(2, 13, 2)
    x_wait(7, 0, 2)
    k_send(3, 0, 2)
    x_wait(8, 15, 1)
    k_send(4, 15, 1)
    for i in range(4):
        arrived(ca.at[lax.rem(y + 4 - i, 4) * 2 + 1 - c], c_r.at[0, 3 + i], sib)
        arrived(cb.at[lax.rem(x + 4 - i, 4) * 2 + 1 - c], c_r.at[1, 3 + i], sib)

    d = lax.broadcasted_iota(jnp.int32, (256, 256), 0)
    other = d // 64
    zz = lax.rem(d // 4, 4) * 4 + lax.rem(d // 16, 4)
    p = lax.rem(d, 4)
    lane = lax.broadcasted_iota(jnp.int32, (1, 128), 1) // 32

    def spread(ref):
        parts = []
        for h in range(2):
            row = ref[4 * h][0:1, :]
            for j in (1, 2, 3):
                row = jnp.where(lane == j, ref[4 * h + j][0:1, :], row)
            parts.append(row)
        return jnp.concatenate(parts, axis=1)

    want_a = ((other * 16 + zz) * 2 + c) * 16 + y * 4 + p
    sel_a = (spread(ca) == want_a).astype(jnp.bfloat16)
    want_b = ((x * 16 + zz) * 2 + c) * 16 + other * 4 + p
    sel_b = (spread(cb) == want_b).astype(jnp.bfloat16)

    k_wait(0, 4, 9)
    k_wait(1, 2, 2)
    k_wait(2, 13, 2)
    k_wait(3, 0, 2)
    k_wait(4, 15, 1)

    def product(q, carry):
        parts = []
        for t in range(4):
            cd = cd_ref[q * 4 + t]
            hr = cd // 4
            slot = lax.rem(lax.rem(hr // 2, 16) - z + 24, 16)
            parts.append(amp[((lax.rem(hr, 2) * 4 + hr // 32) * 16 + slot) * 4 + lax.rem(cd, 4)])
        a = jnp.concatenate(parts, axis=1)
        o = lax.dot_general(a, wbuf[q], (((1,), (1,)), ((), ())), preferred_element_type=jnp.float32)
        osc[pl.ds(pl.multiple_of(q * 32, 32), 32), :] = o
        return carry

    def mine(h, j):
        ref, me = ((xa, y), (xb, x))[h]
        return lambda i: ref.at[lax.rem(me + 4 - i, 4) * 2 + c, pl.ds(j * 16, 16), :]

    def theirs(h, j, i):
        ref, me = ((xa, y), (xb, x))[h]
        return ref.at[lax.rem(me + 4 - i, 4) * 2 + 1 - c, pl.ds(j * 16, 16), :]

    for j in range(2):
        lax.fori_loop(j * 16, j * 16 + 16, product, 0, unroll=4)
        for h in range(2):
            own = mine(h, j)(0)
            for r in range(16):
                v = osc[pl.ds(j * 512 + h * 16 + r, 16, stride=32), :]
                own[:, r * 128 : (r + 1) * 128] = v.astype(jnp.bfloat16)
            for i in (1, 2, 3):
                to = dev(x, y + i, z, c) if h == 0 else dev(x + i, y, z, c)
                send(own, own, p_s.at[h, j, i - 1], p_r.at[h, j, i - 1], to)
            send(own, own, p_s.at[h, j, 3], p_r.at[h, j, 3], sib)
    for h in range(2):
        for j in range(2):
            for i in (1, 2, 3):
                got = mine(h, j)(i)
                arrived(got, p_r.at[h, j, i - 1], sib)
                send(got, got, p_s.at[h, j, 3 + i], p_r.at[h, j, 3 + i], sib)

    def exchange(h, k, sel, src):
        def part(n, carry):
            lanes = pl.ds(pl.multiple_of(k * LANES + n * 256, 256), 256)
            v = src[:, :, lanes].reshape(256, 256)
            t = jnp.dot(sel, v, preferred_element_type=jnp.float32).astype(jnp.bfloat16)
            sd[h, k, :, :, pl.ds(pl.multiple_of(n * 256, 256), 256)] = t.reshape(4, 64, 256)
            return carry

        lax.fori_loop(0, LANES // 256, part, 0, unroll=2)
        for i in (1, 2, 3):
            to = dev(x + i, y, z, c) if h == 0 else dev(x, y + i, z, c)
            me = x if h == 0 else y
            send(sd.at[h, k, lax.rem(me + i, 4)], rd.at[h, k, i - 1], q_s.at[h, k, i - 1], q_r.at[h, k, i - 1], to)

    b4 = lax.rem(z, 4)
    a4 = z // 4

    def gathered(h, k):
        own = x if h == 0 else y
        for i in range(3):
            arrived(rd.at[h, k, i], q_r.at[h, k, i], sib)

        def part(n, carry):
            lanes = pl.ds(pl.multiple_of(n * 256, 256), 256)
            t = sd[h, k, own, :, lanes].astype(jnp.float32)
            for i in range(3):
                t = t + rd[h, k, i, :, lanes].astype(jnp.float32)
            se[h, k, :, :, lanes] = t.astype(jnp.bfloat16).reshape(4, 16, 256)
            return carry

        lax.fori_loop(0, LANES // 256, part, 0)
        for i, step in enumerate((1, -1, 2 * (2 * h - 1))):
            to = lax.rem(b4 + step + 4, 4)
            send(se.at[h, k, to], re.at[h, k, i], e_s.at[h, k, i], e_r.at[h, k, i], dev(x, y, z + step, c))

    def fours(h, k):
        for i in range(3):
            arrived(re.at[h, k, i], e_r.at[h, k, i], sib)
        parts = []
        for u in range(4):
            lanes = slice(u * 256, (u + 1) * 256)
            t = se[h, k, b4, :, lanes].astype(jnp.float32)
            for i in range(3):
                t = t + re[h, k, i, :, lanes].astype(jnp.float32)
            parts.append(t)
        for w in range(4):
            v = jnp.concatenate([t[w * 4 : (w + 1) * 4, :] for t in parts], axis=0)
            sf[h, k, w] = v.astype(jnp.bfloat16)
        for i in (1, 2, 3):
            to = lax.rem(a4 + i, 4)
            send(sf.at[h, k, to], rf.at[h, k, i - 1], f_s.at[h, k, i - 1], f_r.at[h, k, i - 1], dev(x, y, z + 4 * i, c))

    def finish(h, k):
        t = sf[h, k, a4].astype(jnp.float32)
        for i in range(3):
            arrived(rf.at[h, k, i], f_r.at[h, k, i], sib)
            t = t + rf[h, k, i].astype(jnp.float32)
        for u in range(4):
            at = h * HALF + k * LANES + u * 256
            out_ref[:, at : at + 256] = t[u * 4 : (u + 1) * 4, :]

    chunks = [(h, k) for k in range(2) for h in range(2)]
    for h, k in chunks:
        if k == 0:
            for j in range(2):
                for i in range(4):
                    arrived(theirs(h, j, i), p_r.at[h, j, 3 + i], sib)
        exchange(h, k, (sel_a, sel_b)[h], (xa, xb)[h])
    for stage in (gathered, fours, finish):
        for h, k in chunks:
            stage(h, k)

    for cp in sent:
        cp.wait_send()


def per_device(tiles, integral_cd_tile, part_dest, partial_row_place, amplitudes, residual_in):
    bf16, f32, i32, dma = jnp.bfloat16, jnp.float32, jnp.int32, pltpu.SemaphoreType.DMA
    hbm = pl.BlockSpec(memory_space=pltpu.HBM)
    ladder = pl.pallas_call(
        ladder_kernel,
        out_shape=jax.ShapeDtypeStruct((4, 4096), f32),
        in_specs=[hbm] * 5,
        out_specs=pl.BlockSpec(memory_space=pltpu.VMEM),
        scratch_shapes=[
            pltpu.SMEM((128,), i32),
            pltpu.VMEM((1, 32), i32),
            pltpu.VMEM((1, 32), i32),
            pltpu.VMEM((4, 4096), bf16),
            pltpu.VMEM((512, 32, 128), bf16),
            pltpu.VMEM((128, 4096), bf16),
            pltpu.VMEM((4096, 128), f32),
            pltpu.VMEM((32, 128, 512), bf16),
            pltpu.VMEM((1024, 128), f32),
            pltpu.VMEM((8, 32, HALF), bf16),
            pltpu.VMEM((8, 32, HALF), bf16),
            pltpu.VMEM((8, 8, 128), i32),
            pltpu.VMEM((8, 8, 128), i32),
            pltpu.VMEM((2, 2, 4, 64, LANES), bf16),
            pltpu.VMEM((2, 2, 3, 64, LANES), bf16),
            pltpu.VMEM((2, 2, 4, 16, LANES), bf16),
            pltpu.VMEM((2, 2, 3, 16, LANES), bf16),
            pltpu.VMEM((2, 2, 4, 16, 256), bf16),
            pltpu.VMEM((2, 2, 3, 16, 256), bf16),
            dma((5,)),
            dma((16,)), dma((16,)),
            dma((9, 3)), dma((9, 3)),
            dma((5, 4)), dma((5, 4)),
            dma((2, 7)), dma((2, 7)),
            dma((2, 2, 7)), dma((2, 2, 7)),
            dma((2, 2, 3)), dma((2, 2, 3)),
            dma((2, 2, 3)), dma((2, 2, 3)),
            dma((2, 2, 3)), dma((2, 2, 3)),
        ],
        compiler_params=pltpu.CompilerParams(
            collective_id=0, has_side_effects=True, vmem_limit_bytes=63 << 20
        ),
    )(
        integral_cd_tile,
        part_dest.reshape(1, PAB),
        partial_row_place.reshape(1, PAB),
        amplitudes.reshape(4, 4096),
        tiles,
    )
    return residual_in + ladder[None]


def solution(mesh):
    return jax.shard_map(
        per_device,
        mesh=mesh,
        in_specs=(
            P(("rows", "cols"), None),
            P(("rows", "cols")),
            P(("rows", "cols"), None),
            P(("rows", "cols")),
            P("cols", "rows", None),
            P("rows", "cols", None),
        ),
        out_specs=P("rows", "cols", None),
        check_vma=False,
    )
```

```python
import jax
import jax.numpy as jnp
from jax import lax
from jax.experimental import pallas as pl
from jax.experimental.pallas import tpu as pltpu
from jax.sharding import PartitionSpec as P

PAB = 32
HALF = 2048
LANES = 1024
MESH = pl.DeviceIdType.MESH


def coords():
    r = lax.axis_index("rows")
    y = lax.axis_index("cols")
    return r // 32, y, lax.rem(r // 2, 16), lax.rem(r, 2)


def dev(x, y, z, c):
    return ((lax.rem(x + 4, 4) * 16 + lax.rem(z + 16, 16)) * 2 + lax.rem(c, 2), lax.rem(y + 4, 4))


def ladder_kernel(
    cd_hbm, dest_hbm, place_hbm, amp_hbm, tiles_hbm, out_ref,
    cd_ref, dest, place, amp4, amp, tv, tsc, wbuf, osc, xa, xb, ca, cb, sd, rd, se, re, sf, rf,
    in_sem, z_s, z_r, o_s, o_r, g_s, g_r, x_s, x_r, k_s, k_r, c_s, c_r, p_s, p_r, q_s, q_r, e_s, e_r, f_s, f_r,
):
    x, y, z, c = coords()
    sent = []

    def send(src, dst, ss, rs, to):
        cp = pltpu.make_async_remote_copy(
            src_ref=src, dst_ref=dst, send_sem=ss, recv_sem=rs, device_id=to, device_id_type=MESH
        )
        cp.start()
        sent.append(cp)

    def arrived(dst, rs, to):
        pltpu.make_async_remote_copy(
            src_ref=dst, dst_ref=dst, send_sem=rs, recv_sem=rs, device_id=to, device_id_type=MESH
        ).wait_recv()

    sib = dev(x, y, z, c + 1)
    barrier = pltpu.get_barrier_semaphore()
    friends = [dev(x, y, z + d, c) for d in (1, -1, 2, -2)]
    friends += [dev(x + d, y, z, c) for d in (1, 2, 3)]
    friends += [dev(x, y + d, z, c) for d in (1, 2, 3)]
    friends += [sib]
    for t in friends:
        pl.semaphore_signal(barrier, inc=1, device_id=t, device_id_type=MESH)
    loads = []
    for i, (src, dst) in enumerate(
        ((amp_hbm, amp4), (dest_hbm, dest), (place_hbm, place), (cd_hbm, cd_ref), (tiles_hbm, tv))
    ):
        loads.append(pltpu.make_async_copy(src, dst, in_sem.at[i]))
        loads[-1].start()

    def block(xx, slot, n=1, cc=None):
        cc = c if cc is None else cc
        return amp.at[pl.ds(((cc * 4 + xx) * 16 + slot) * 3, 3 * n)]

    def first(slot, n=1, cc=None):
        cc = c if cc is None else cc
        return amp.at[pl.ds(384 + (cc * 16 + slot) * 4, 4 * n)]

    for i in range(3):
        loads[i].wait()
    v = amp4[...].astype(jnp.float32)
    for l in range(32):
        osc[pl.ds(l, 4, stride=32), :] = v[:, l * 128 : (l + 1) * 128]
    v = osc[0:128, :].reshape(4, 32, 128).astype(jnp.bfloat16)
    one = 384 + (c * 16 + 8) * 4 + x
    amp[one] = v[0]
    amp[pl.ds(((c * 4 + x) * 16 + 8) * 3, 3)] = v[1:4]
    code = dest[...] * 16 + place[...]
    code = jnp.broadcast_to(jnp.concatenate([code] * 4, axis=1), (8, 128))
    ca[y * 2 + c] = code
    cb[x * 2 + c] = code
    pl.semaphore_wait(barrier, len(friends))

    def z_send(kind, slot, step):
        to = slot - step
        src, dst = (first(slot), first(to)) if kind else (block(x, slot), block(x, to))
        send(src, dst, z_s.at[kind, to], z_r.at[kind, to], dev(x, y, z + step, c))

    def z_wait(kind, slot):
        arrived(first(slot) if kind else block(x, slot), z_r.at[kind, slot], sib)

    def z_relay(kind, left, right):
        z_wait(kind, left)
        z_send(kind, left, 2)
        z_send(kind, left, 1)
        z_wait(kind, right)
        if right < 14:
            z_send(kind, right, -2)
        z_send(kind, right, -1)

    def x_send(g, slot, n):
        for i in (1, 2, 3):
            send(block(x, slot, n), block(x, slot, n), x_s.at[g, i - 1], x_r.at[g, i - 1], dev(x + i, y, z, c))

    def x_wait(g, slot, n):
        for i in (1, 2, 3):
            arrived(block(lax.rem(x + 4 - i, 4), slot, n), x_r.at[g, i - 1], sib)

    def k_send(g, slot, n):
        for i in range(4):
            xs = lax.rem(x + 4 - i, 4)
            send(block(xs, slot, n), block(xs, slot, n), k_s.at[g, i], k_r.at[g, i], sib)

    def k_wait(g, slot, n):
        for i in range(4):
            xs = lax.rem(x + 4 - i, 4)
            arrived(block(xs, slot, n, 1 - c), k_r.at[g, i], sib)

    def f_send(g, slot, n):
        send(first(slot, n), first(slot, n), g_s.at[g], g_r.at[g], sib)

    def f_wait(g, slot, n):
        arrived(first(slot, n, 1 - c), g_r.at[g], sib)

    for i in (1, 2, 3):
        send(amp.at[one], amp.at[one], o_s.at[i - 1], o_r.at[i - 1], dev(x + i, y, z, c))
    for step in (2, -2, 1, -1):
        z_send(0, 8, step)
    x_send(0, 8, 1)
    for i in (1, 2, 3):
        me = ca.at[y * 2 + c]
        send(me, me, c_s.at[0, i - 1], c_r.at[0, i - 1], dev(x, y + i, z, c))
        me = cb.at[x * 2 + c]
        send(me, me, c_s.at[1, i - 1], c_r.at[1, i - 1], dev(x + i, y, z, c))

    rows = lax.broadcasted_iota(jnp.int32, (128, 64), 0)
    cols = lax.broadcasted_iota(jnp.int32, (128, 64), 1)
    par = rows // 64
    ab = lax.rem(rows, 64)
    take = (cols == ab // 2 + 32 * (lax.rem(ab, 2) ^ par)).astype(jnp.bfloat16)
    keep = lax.rem(lax.broadcasted_iota(jnp.int32, (128, 512), 1), 128) // 64 == (
        lax.broadcasted_iota(jnp.int32, (128, 512), 0) // 64
    )

    def relayout(j, carry):
        base = pl.multiple_of(j * 16, 16)
        v = tv[pl.ds(base, 16), :].astype(jnp.float32)
        for l in range(32):
            tsc[pl.ds(base * 32 + l, 16, stride=32), :] = v[:, l * 128 : (l + 1) * 128]
        return carry

    def build(q, carry):
        both = []
        for t in range(4):
            b2 = tsc[pl.ds(pl.multiple_of((q * 4 + t) * 32, 32), 32), :]
            both.append(jnp.concatenate([b2, pltpu.roll(b2, 64, 1)], axis=0))
        r = jnp.concatenate(both, axis=1).astype(jnp.bfloat16)
        g = jnp.dot(take, r, preferred_element_type=jnp.float32)
        wbuf[q] = jnp.where(keep, g, 0.0).astype(jnp.bfloat16)
        return carry

    def prep(lo, hi):
        lax.fori_loop(lo // 4, hi // 4, relayout, 0)
        lax.fori_loop(lo, hi, build, 0)

    loads[3].wait()
    loads[4].wait()
    prep(0, 4)
    for i in (1, 2, 3):
        got = amp.at[384 + (c * 16 + 8) * 4 + lax.rem(x + 4 - i, 4)]
        arrived(got, o_r.at[i - 1], sib)
    for step in (2, -2, 1, -1):
        z_send(1, 8, step)
    z_relay(0, 6, 10)
    z_wait(0, 7)
    x_send(1, 6, 2)
    z_wait(0, 9)
    x_send(2, 9, 2)
    prep(4, 8)
    z_relay(1, 6, 10)
    prep(8, 12)
    z_relay(0, 4, 12)
    z_wait(0, 5)
    x_send(3, 4, 2)
    z_wait(0, 11)
    x_send(4, 11, 2)
    prep(12, 16)
    z_relay(1, 4, 12)
    prep(16, 20)
    z_relay(0, 2, 14)
    z_wait(0, 3)
    x_send(5, 2, 2)
    z_wait(0, 13)
    x_send(6, 13, 2)
    prep(20, 24)
    z_relay(1, 2, 14)
    for i in (1, 2, 3):
        arrived(ca.at[lax.rem(y + 4 - i, 4) * 2 + c], c_r.at[0, i - 1], sib)
        arrived(cb.at[lax.rem(x + 4 - i, 4) * 2 + c], c_r.at[1, i - 1], sib)
    for i in range(4):
        t = ca.at[lax.rem(y + 4 - i, 4) * 2 + c]
        send(t, t, c_s.at[0, 3 + i], c_r.at[0, 3 + i], sib)
        t = cb.at[lax.rem(x + 4 - i, 4) * 2 + c]
        send(t, t, c_s.at[1, 3 + i], c_r.at[1, 3 + i], sib)
    z_wait(0, 0)
    z_wait(0, 1)
    x_send(7, 0, 2)
    z_wait(0, 15)
    x_send(8, 15, 1)
    prep(24, 32)
    for slot in (5, 7, 9, 11):
        z_wait(1, slot)
    f_send(0, 4, 9)
    x_wait(0, 8, 1)
    x_wait(1, 6, 2)
    x_wait(2, 9, 2)
    x_wait(3, 4, 2)
    x_wait(4, 11, 2)
    k_send(0, 4, 9)
    z_wait(1, 3)
    f_send(1, 2, 2)
    z_wait(1, 13)
    f_send(2, 13, 2)
    z_wait(1, 0)
    z_wait(1, 1)
    f_send(3, 0, 2)
    z_wait(1, 15)
    f_send(4, 15, 1)
    x_wait(5, 2, 2)
    k_send(1, 2, 2)
    x_wait(6, 13, 2)
    k_send(2, 13, 2)
    x_wait(7, 0, 2)
    k_send(3, 0, 2)
    x_wait(8, 15, 1)
    k_send(4, 15, 1)
    for i in range(4):
        arrived(ca.at[lax.rem(y + 4 - i, 4) * 2 + 1 - c], c_r.at[0, 3 + i], sib)
        arrived(cb.at[lax.rem(x + 4 - i, 4) * 2 + 1 - c], c_r.at[1, 3 + i], sib)

    d = lax.broadcasted_iota(jnp.int32, (256, 256), 0)
    other = d // 64
    zz = lax.rem(d // 4, 4) * 4 + lax.rem(d // 16, 4)
    p = lax.rem(d, 4)
    lane = lax.broadcasted_iota(jnp.int32, (1, 128), 1) // 32

    def spread(ref):
        parts = []
        for h in range(2):
            row = ref[4 * h][0:1, :]
            for j in (1, 2, 3):
                row = jnp.where(lane == j, ref[4 * h + j][0:1, :], row)
            parts.append(row)
        return jnp.concatenate(parts, axis=1)

    want_a = ((other * 16 + zz) * 2 + c) * 16 + y * 4 + p
    sel_a = (spread(ca) == want_a).astype(jnp.bfloat16)
    want_b = ((x * 16 + zz) * 2 + c) * 16 + other * 4 + p
    sel_b = (spread(cb) == want_b).astype(jnp.bfloat16)

    for g, slot, n in ((0, 4, 9), (1, 2, 2), (2, 13, 2), (3, 0, 2), (4, 15, 1)):
        f_wait(g, slot, n)
        k_wait(g, slot, n)

    def product(q, carry):
        parts = []
        for t in range(4):
            cd = cd_ref[q * 4 + t]
            hr = cd // 4
            slot = lax.rem(lax.rem(hr // 2, 16) - z + 24, 16)
            xx, cc, at = hr // 32, lax.rem(hr, 2), lax.rem(cd, 4)
            three = ((cc * 4 + xx) * 16 + slot) * 3 + at - 1
            parts.append(amp[jnp.where(at == 0, 384 + (cc * 16 + slot) * 4 + xx, three)])
        a = jnp.concatenate(parts, axis=1)
        o = lax.dot_general(a, wbuf[q], (((1,), (1,)), ((), ())), preferred_element_type=jnp.float32)
        osc[pl.ds(pl.multiple_of(q * 32, 32), 32), :] = o
        return carry

    def mine(h, j):
        ref, me = ((xa, y), (xb, x))[h]
        return lambda i: ref.at[lax.rem(me + 4 - i, 4) * 2 + c, pl.ds(j * 16, 16), :]

    def theirs(h, j, i):
        ref, me = ((xa, y), (xb, x))[h]
        return ref.at[lax.rem(me + 4 - i, 4) * 2 + 1 - c, pl.ds(j * 16, 16), :]

    for j in range(2):
        lax.fori_loop(j * 16, j * 16 + 16, product, 0, unroll=4)
        for h in range(2):
            own = mine(h, j)(0)
            for r in range(16):
                v = osc[pl.ds(j * 512 + h * 16 + r, 16, stride=32), :]
                own[:, r * 128 : (r + 1) * 128] = v.astype(jnp.bfloat16)
            for i in (1, 2, 3):
                to = dev(x, y + i, z, c) if h == 0 else dev(x + i, y, z, c)
                send(own, own, p_s.at[h, j, i - 1], p_r.at[h, j, i - 1], to)
            send(own, own, p_s.at[h, j, 3], p_r.at[h, j, 3], sib)
    for h in range(2):
        for j in range(2):
            for i in (1, 2, 3):
                got = mine(h, j)(i)
                arrived(got, p_r.at[h, j, i - 1], sib)
                send(got, got, p_s.at[h, j, 3 + i], p_r.at[h, j, 3 + i], sib)

    def exchange(h, k, sel, src):
        def part(n, carry):
            lanes = pl.ds(pl.multiple_of(k * LANES + n * 256, 256), 256)
            v = src[:, :, lanes].reshape(256, 256)
            t = jnp.dot(sel, v, preferred_element_type=jnp.float32).astype(jnp.bfloat16)
            sd[h, k, :, :, pl.ds(pl.multiple_of(n * 256, 256), 256)] = t.reshape(4, 64, 256)
            return carry

        lax.fori_loop(0, LANES // 256, part, 0, unroll=2)
        for i in (1, 2, 3):
            to = dev(x + i, y, z, c) if h == 0 else dev(x, y + i, z, c)
            me = x if h == 0 else y
            send(sd.at[h, k, lax.rem(me + i, 4)], rd.at[h, k, i - 1], q_s.at[h, k, i - 1], q_r.at[h, k, i - 1], to)

    b4 = lax.rem(z, 4)
    a4 = z // 4

    def gathered(h, k):
        own = x if h == 0 else y
        for i in range(3):
            arrived(rd.at[h, k, i], q_r.at[h, k, i], sib)

        def part(n, carry):
            lanes = pl.ds(pl.multiple_of(n * 256, 256), 256)
            t = sd[h, k, own, :, lanes].astype(jnp.float32)
            for i in range(3):
                t = t + rd[h, k, i, :, lanes].astype(jnp.float32)
            se[h, k, :, :, lanes] = t.astype(jnp.bfloat16).reshape(4, 16, 256)
            return carry

        lax.fori_loop(0, LANES // 256, part, 0)
        for i, step in enumerate((1, -1, 2 * (2 * h - 1))):
            to = lax.rem(b4 + step + 4, 4)
            send(se.at[h, k, to], re.at[h, k, i], e_s.at[h, k, i], e_r.at[h, k, i], dev(x, y, z + step, c))

    def fours(h, k):
        for i in range(3):
            arrived(re.at[h, k, i], e_r.at[h, k, i], sib)
        parts = []
        for u in range(4):
            lanes = slice(u * 256, (u + 1) * 256)
            t = se[h, k, b4, :, lanes].astype(jnp.float32)
            for i in range(3):
                t = t + re[h, k, i, :, lanes].astype(jnp.float32)
            parts.append(t)
        for w in range(4):
            v = jnp.concatenate([t[w * 4 : (w + 1) * 4, :] for t in parts], axis=0)
            sf[h, k, w] = v.astype(jnp.bfloat16)
        for i in (1, 2, 3):
            to = lax.rem(a4 + i, 4)
            send(sf.at[h, k, to], rf.at[h, k, i - 1], f_s.at[h, k, i - 1], f_r.at[h, k, i - 1], dev(x, y, z + 4 * i, c))

    def finish(h, k):
        t = sf[h, k, a4].astype(jnp.float32)
        for i in range(3):
            arrived(rf.at[h, k, i], f_r.at[h, k, i], sib)
            t = t + rf[h, k, i].astype(jnp.float32)
        for u in range(4):
            at = h * HALF + k * LANES + u * 256
            out_ref[:, at : at + 256] = t[u * 4 : (u + 1) * 4, :]

    chunks = [(h, k) for k in range(2) for h in range(2)]
    for h, k in chunks:
        if k == 0:
            for j in range(2):
                for i in range(4):
                    arrived(theirs(h, j, i), p_r.at[h, j, 3 + i], sib)
        exchange(h, k, (sel_a, sel_b)[h], (xa, xb)[h])
    for stage in (gathered, fours, finish):
        for h, k in chunks:
            stage(h, k)

    for cp in sent:
        cp.wait_send()


def per_device(tiles, integral_cd_tile, part_dest, partial_row_place, amplitudes, residual_in):
    bf16, f32, i32, dma = jnp.bfloat16, jnp.float32, jnp.int32, pltpu.SemaphoreType.DMA
    hbm = pl.BlockSpec(memory_space=pltpu.HBM)
    ladder = pl.pallas_call(
        ladder_kernel,
        out_shape=jax.ShapeDtypeStruct((4, 4096), f32),
        in_specs=[hbm] * 5,
        out_specs=pl.BlockSpec(memory_space=pltpu.VMEM),
        scratch_shapes=[
            pltpu.SMEM((128,), i32),
            pltpu.VMEM((1, 32), i32),
            pltpu.VMEM((1, 32), i32),
            pltpu.VMEM((4, 4096), bf16),
            pltpu.VMEM((512, 32, 128), bf16),
            pltpu.VMEM((128, 4096), bf16),
            pltpu.VMEM((4096, 128), f32),
            pltpu.VMEM((32, 128, 512), bf16),
            pltpu.VMEM((1024, 128), f32),
            pltpu.VMEM((8, 32, HALF), bf16),
            pltpu.VMEM((8, 32, HALF), bf16),
            pltpu.VMEM((8, 8, 128), i32),
            pltpu.VMEM((8, 8, 128), i32),
            pltpu.VMEM((2, 2, 4, 64, LANES), bf16),
            pltpu.VMEM((2, 2, 3, 64, LANES), bf16),
            pltpu.VMEM((2, 2, 4, 16, LANES), bf16),
            pltpu.VMEM((2, 2, 3, 16, LANES), bf16),
            pltpu.VMEM((2, 2, 4, 16, 256), bf16),
            pltpu.VMEM((2, 2, 3, 16, 256), bf16),
            dma((5,)),
            dma((2, 16)), dma((2, 16)),
            dma((3,)), dma((3,)),
            dma((5,)), dma((5,)),
            dma((9, 3)), dma((9, 3)),
            dma((5, 4)), dma((5, 4)),
            dma((2, 7)), dma((2, 7)),
            dma((2, 2, 7)), dma((2, 2, 7)),
            dma((2, 2, 3)), dma((2, 2, 3)),
            dma((2, 2, 3)), dma((2, 2, 3)),
            dma((2, 2, 3)), dma((2, 2, 3)),
        ],
        compiler_params=pltpu.CompilerParams(
            collective_id=0, has_side_effects=True, vmem_limit_bytes=63 << 20
        ),
    )(
        integral_cd_tile,
        part_dest.reshape(1, PAB),
        partial_row_place.reshape(1, PAB),
        amplitudes.reshape(4, 4096),
        tiles,
    )
    return residual_in + ladder[None]


def solution(mesh):
    return jax.shard_map(
        per_device,
        mesh=mesh,
        in_specs=(
            P(("rows", "cols"), None),
            P(("rows", "cols")),
            P(("rows", "cols"), None),
            P(("rows", "cols")),
            P("cols", "rows", None),
            P("rows", "cols", None),
        ),
        out_specs=P("rows", "cols", None),
        check_vma=False,
    )
```

```python
import jax
import jax.numpy as jnp
from jax import lax
from jax.experimental import pallas as pl
from jax.experimental.pallas import tpu as pltpu
from jax.sharding import PartitionSpec as P

PAB = 32
HALF = 2048
LANES = 1024
MESH = pl.DeviceIdType.MESH


def coords():
    r = lax.axis_index("rows")
    y = lax.axis_index("cols")
    return r // 32, y, lax.rem(r // 2, 16), lax.rem(r, 2)


def dev(x, y, z, c):
    return ((lax.rem(x + 4, 4) * 16 + lax.rem(z + 16, 16)) * 2 + lax.rem(c, 2), lax.rem(y + 4, 4))


def ladder_kernel(
    cd_hbm, dest_hbm, place_hbm, amp_hbm, tiles_hbm, out_ref,
    cd_ref, dest, place, amp4, amp, tv, tsc, wbuf, osc, xa, xb, ca, cb, sd, rd, se, re, kept, sf, rf,
    in_sem, z_s, z_r, o_s, o_r, g_s, g_r, x_s, x_r, k_s, k_r, c_s, c_r, p_s, p_r, q_s, q_r, e_s, e_r, f_s, f_r,
):
    x, y, z, c = coords()
    sent = []

    def send(src, dst, ss, rs, to):
        cp = pltpu.make_async_remote_copy(
            src_ref=src, dst_ref=dst, send_sem=ss, recv_sem=rs, device_id=to, device_id_type=MESH
        )
        cp.start()
        sent.append(cp)

    def arrived(dst, rs, to):
        pltpu.make_async_remote_copy(
            src_ref=dst, dst_ref=dst, send_sem=rs, recv_sem=rs, device_id=to, device_id_type=MESH
        ).wait_recv()

    sib = dev(x, y, z, c + 1)
    barrier = pltpu.get_barrier_semaphore()
    friends = [dev(x, y, z + d, c) for d in (1, -1, 2, -2)]
    friends += [dev(x + d, y, z, c) for d in (1, 2, 3)]
    friends += [dev(x, y + d, z, c) for d in (1, 2, 3)]
    friends += [sib]
    for t in friends:
        pl.semaphore_signal(barrier, inc=1, device_id=t, device_id_type=MESH)
    loads = []
    for i, (src, dst) in enumerate(
        ((amp_hbm, amp4), (dest_hbm, dest), (place_hbm, place), (cd_hbm, cd_ref), (tiles_hbm, tv))
    ):
        loads.append(pltpu.make_async_copy(src, dst, in_sem.at[i]))
        loads[-1].start()

    def block(xx, slot, n=1, cc=None):
        cc = c if cc is None else cc
        return amp.at[pl.ds(((cc * 4 + xx) * 16 + slot) * 3, 3 * n)]

    def first(slot, n=1, cc=None):
        cc = c if cc is None else cc
        return amp.at[pl.ds(384 + (cc * 16 + slot) * 4, 4 * n)]

    for i in range(3):
        loads[i].wait()
    v = amp4[...].astype(jnp.float32)
    for l in range(32):
        osc[pl.ds(l, 4, stride=32), :] = v[:, l * 128 : (l + 1) * 128]
    v = osc[0:128, :].reshape(4, 32, 128).astype(jnp.bfloat16)
    one = 384 + (c * 16 + 8) * 4 + x
    amp[one] = v[0]
    amp[pl.ds(((c * 4 + x) * 16 + 8) * 3, 3)] = v[1:4]
    code = dest[...] * 16 + place[...]
    code = jnp.broadcast_to(jnp.concatenate([code] * 4, axis=1), (8, 128))
    ca[y * 2 + c] = code
    cb[x * 2 + c] = code
    pl.semaphore_wait(barrier, len(friends))

    def z_send(kind, slot, step):
        to = slot - step
        src, dst = (first(slot), first(to)) if kind else (block(x, slot), block(x, to))
        send(src, dst, z_s.at[kind, to], z_r.at[kind, to], dev(x, y, z + step, c))

    def z_wait(kind, slot):
        arrived(first(slot) if kind else block(x, slot), z_r.at[kind, slot], sib)

    def z_relay(kind, left, right):
        z_wait(kind, left)
        z_send(kind, left, 2)
        z_send(kind, left, 1)
        z_wait(kind, right)
        if right < 14:
            z_send(kind, right, -2)
        z_send(kind, right, -1)

    def x_send(g, slot, n):
        for i in (1, 2, 3):
            send(block(x, slot, n), block(x, slot, n), x_s.at[g, i - 1], x_r.at[g, i - 1], dev(x + i, y, z, c))

    def k_send(g, slot, n, i, wait=()):
        xs = lax.rem(x + 4 - i, 4)
        if i > 0:
            for w, ws, wn in wait:
                arrived(block(xs, ws, wn), x_r.at[w, i - 1], sib)
        send(block(xs, slot, n), block(xs, slot, n), k_s.at[g, i], k_r.at[g, i], sib)

    def k_wait(g, slot, n):
        for i in range(4):
            xs = lax.rem(x + 4 - i, 4)
            arrived(block(xs, slot, n, 1 - c), k_r.at[g, i], sib)

    def f_send(g, slot, n):
        send(first(slot, n), first(slot, n), g_s.at[g], g_r.at[g], sib)

    def f_wait(g, slot, n):
        arrived(first(slot, n, 1 - c), g_r.at[g], sib)

    for i in (1, 2, 3):
        send(amp.at[one], amp.at[one], o_s.at[i - 1], o_r.at[i - 1], dev(x + i, y, z, c))
    for step in (2, -2, 1, -1):
        z_send(0, 8, step)
    x_send(0, 8, 1)
    for i in (1, 2, 3):
        me = ca.at[y * 2 + c]
        send(me, me, c_s.at[0, i - 1], c_r.at[0, i - 1], dev(x, y + i, z, c))
        me = cb.at[x * 2 + c]
        send(me, me, c_s.at[1, i - 1], c_r.at[1, i - 1], dev(x + i, y, z, c))

    rows = lax.broadcasted_iota(jnp.int32, (128, 64), 0)
    cols = lax.broadcasted_iota(jnp.int32, (128, 64), 1)
    par = rows // 64
    ab = lax.rem(rows, 64)
    take = (cols == ab // 2 + 32 * (lax.rem(ab, 2) ^ par)).astype(jnp.bfloat16)
    keep = lax.rem(lax.broadcasted_iota(jnp.int32, (128, 512), 1), 128) // 64 == (
        lax.broadcasted_iota(jnp.int32, (128, 512), 0) // 64
    )

    def relayout(j, carry):
        base = pl.multiple_of(j * 16, 16)
        v = tv[pl.ds(base, 16), :].astype(jnp.float32)
        for l in range(32):
            tsc[pl.ds(base * 32 + l, 16, stride=32), :] = v[:, l * 128 : (l + 1) * 128]
        return carry

    def build(q, carry):
        both = []
        for t in range(4):
            b2 = tsc[pl.ds(pl.multiple_of((q * 4 + t) * 32, 32), 32), :]
            both.append(jnp.concatenate([b2, pltpu.roll(b2, 64, 1)], axis=0))
        r = jnp.concatenate(both, axis=1).astype(jnp.bfloat16)
        g = jnp.dot(take, r, preferred_element_type=jnp.float32)
        wbuf[q] = jnp.where(keep, g, 0.0).astype(jnp.bfloat16)
        return carry

    def prep(lo, hi):
        lax.fori_loop(lo // 4, hi // 4, relayout, 0)
        lax.fori_loop(lo, hi, build, 0, unroll=4)

    loads[3].wait()
    loads[4].wait()
    prep(0, 4)
    for i in (1, 2, 3):
        got = amp.at[384 + (c * 16 + 8) * 4 + lax.rem(x + 4 - i, 4)]
        arrived(got, o_r.at[i - 1], sib)
    for step in (2, -2, 1, -1):
        z_send(1, 8, step)
    z_relay(0, 6, 10)
    z_wait(0, 7)
    x_send(1, 6, 2)
    z_wait(0, 9)
    x_send(2, 9, 2)
    prep(4, 8)
    z_relay(1, 6, 10)
    prep(8, 12)
    z_relay(0, 4, 12)
    z_wait(0, 5)
    x_send(3, 4, 2)
    z_wait(0, 11)
    x_send(4, 11, 2)
    prep(12, 16)
    z_relay(1, 4, 12)
    prep(16, 20)
    z_relay(0, 2, 14)
    z_wait(0, 3)
    x_send(5, 2, 2)
    z_wait(0, 13)
    x_send(6, 13, 2)
    prep(20, 24)
    z_relay(1, 2, 14)
    for i in (1, 2, 3):
        arrived(ca.at[lax.rem(y + 4 - i, 4) * 2 + c], c_r.at[0, i - 1], sib)
        arrived(cb.at[lax.rem(x + 4 - i, 4) * 2 + c], c_r.at[1, i - 1], sib)
    for i in range(4):
        t = ca.at[lax.rem(y + 4 - i, 4) * 2 + c]
        send(t, t, c_s.at[0, 3 + i], c_r.at[0, 3 + i], sib)
        t = cb.at[lax.rem(x + 4 - i, 4) * 2 + c]
        send(t, t, c_s.at[1, 3 + i], c_r.at[1, 3 + i], sib)
    z_wait(0, 0)
    z_wait(0, 1)
    x_send(7, 0, 2)
    z_wait(0, 15)
    x_send(8, 15, 1)
    prep(24, 32)
    for slot in (5, 7, 9, 11):
        z_wait(1, slot)
    f_send(0, 4, 9)
    for i in (0, 1, 3, 2):
        k_send(0, 4, 9, i, ((0, 8, 1), (1, 6, 2), (2, 9, 2), (3, 4, 2), (4, 11, 2)))
    for g, slot, n in ((1, 2, 2), (2, 13, 2), (3, 0, 2), (4, 15, 1)):
        k_send(g, slot, n, 0)
    z_wait(1, 3)
    f_send(1, 2, 2)
    z_wait(1, 13)
    f_send(2, 13, 2)
    z_wait(1, 0)
    z_wait(1, 1)
    f_send(3, 0, 2)
    z_wait(1, 15)
    f_send(4, 15, 1)
    for g, slot, n in ((1, 2, 2), (2, 13, 2), (3, 0, 2), (4, 15, 1)):
        for i in (1, 3, 2):
            k_send(g, slot, n, i, ((g + 4, slot, n),))
    for i in range(4):
        arrived(ca.at[lax.rem(y + 4 - i, 4) * 2 + 1 - c], c_r.at[0, 3 + i], sib)
        arrived(cb.at[lax.rem(x + 4 - i, 4) * 2 + 1 - c], c_r.at[1, 3 + i], sib)

    d = lax.broadcasted_iota(jnp.int32, (256, 256), 0)
    other = d // 64
    zz = lax.rem(d // 4, 4) * 4 + lax.rem(d // 16, 4)
    p = lax.rem(d, 4)
    lane = lax.broadcasted_iota(jnp.int32, (1, 128), 1) // 32

    def spread(ref):
        parts = []
        for h in range(2):
            row = ref[4 * h][0:1, :]
            for j in (1, 2, 3):
                row = jnp.where(lane == j, ref[4 * h + j][0:1, :], row)
            parts.append(row)
        return jnp.concatenate(parts, axis=1)

    want_a = ((other * 16 + zz) * 2 + c) * 16 + y * 4 + p
    sel_a = (spread(ca) == want_a).astype(jnp.bfloat16)
    want_b = ((x * 16 + zz) * 2 + c) * 16 + other * 4 + p
    sel_b = (spread(cb) == want_b).astype(jnp.bfloat16)

    for g, slot, n in ((0, 4, 9), (1, 2, 2), (2, 13, 2), (3, 0, 2), (4, 15, 1)):
        f_wait(g, slot, n)
        k_wait(g, slot, n)

    def product(q, carry):
        parts = []
        for t in range(4):
            cd = cd_ref[q * 4 + t]
            hr = cd // 4
            slot = lax.rem(lax.rem(hr // 2, 16) - z + 24, 16)
            xx, cc, at = hr // 32, lax.rem(hr, 2), lax.rem(cd, 4)
            three = ((cc * 4 + xx) * 16 + slot) * 3 + at - 1
            parts.append(amp[jnp.where(at == 0, 384 + (cc * 16 + slot) * 4 + xx, three)])
        a = jnp.concatenate(parts, axis=1)
        o = lax.dot_general(a, wbuf[q], (((1,), (1,)), ((), ())), preferred_element_type=jnp.float32)
        osc[pl.ds(pl.multiple_of(q * 32, 32), 32), :] = o
        return carry

    def mine(h, j):
        ref, me = ((xa, y), (xb, x))[h]
        return lambda i: ref.at[lax.rem(me + 4 - i, 4) * 2 + c, pl.ds(j * 16, 16), :]

    def theirs(h, j, i):
        ref, me = ((xa, y), (xb, x))[h]
        return ref.at[lax.rem(me + 4 - i, 4) * 2 + 1 - c, pl.ds(j * 16, 16), :]

    for j in range(2):
        lax.fori_loop(j * 16, j * 16 + 16, product, 0, unroll=16)
        for h in range(2):
            own = mine(h, j)(0)
            for r in range(16):
                v = osc[pl.ds(j * 512 + h * 16 + r, 16, stride=32), :]
                own[:, r * 128 : (r + 1) * 128] = v.astype(jnp.bfloat16)
            for i in (1, 2, 3):
                to = dev(x, y + i, z, c) if h == 0 else dev(x + i, y, z, c)
                send(own, own, p_s.at[h, j, i - 1], p_r.at[h, j, i - 1], to)
            send(own, own, p_s.at[h, j, 3], p_r.at[h, j, 3], sib)
    for j in range(2):
        for i in (1, 3, 2):
            for h in range(2):
                got = mine(h, j)(i)
                arrived(got, p_r.at[h, j, i - 1], sib)
                send(got, got, p_s.at[h, j, 3 + i], p_r.at[h, j, 3 + i], sib)

    def exchange(h, k, sel, src):
        def part(n, carry):
            lanes = pl.ds(pl.multiple_of(k * LANES + n * 256, 256), 256)
            v = src[:, :, lanes].reshape(256, 256)
            t = jnp.dot(sel, v, preferred_element_type=jnp.float32).astype(jnp.bfloat16)
            sd[h, k, :, :, pl.ds(pl.multiple_of(n * 256, 256), 256)] = t.reshape(4, 64, 256)
            return carry

        lax.fori_loop(0, LANES // 256, part, 0, unroll=2)
        for i in (1, 2, 3):
            to = dev(x + i, y, z, c) if h == 0 else dev(x, y + i, z, c)
            me = x if h == 0 else y
            send(sd.at[h, k, lax.rem(me + i, 4)], rd.at[h, k, i - 1], q_s.at[h, k, i - 1], q_r.at[h, k, i - 1], to)

    b4 = lax.rem(z, 4)
    a4 = z // 4

    def gathered(h, k):
        own = x if h == 0 else y
        for i in range(3):
            arrived(rd.at[h, k, i], q_r.at[h, k, i], sib)

        def part(n, carry):
            lanes = pl.ds(pl.multiple_of(n * 256, 256), 256)
            t = sd[h, k, own, :, lanes].astype(jnp.float32)
            for i in range(3):
                t = t + rd[h, k, i, :, lanes].astype(jnp.float32)
            t = t.reshape(4, 16, 256)
            kept[h, k, :, :, lanes] = t
            se[h, k, :, :, lanes] = t.astype(jnp.bfloat16)
            return carry

        lax.fori_loop(0, LANES // 256, part, 0, unroll=2)
        for i, step in enumerate((1, -1, 2 * (2 * h - 1))):
            to = lax.rem(b4 + step + 4, 4)
            send(se.at[h, k, to], re.at[h, k, i], e_s.at[h, k, i], e_r.at[h, k, i], dev(x, y, z + step, c))

    def fours(h, k):
        for i in range(3):
            arrived(re.at[h, k, i], e_r.at[h, k, i], sib)
        parts = []
        for u in range(4):
            lanes = slice(u * 256, (u + 1) * 256)
            t = kept[h, k, b4, :, lanes]
            for i in range(3):
                t = t + re[h, k, i, :, lanes].astype(jnp.float32)
            parts.append(t)
        for w in range(4):
            v = jnp.concatenate([t[w * 4 : (w + 1) * 4, :] for t in parts], axis=0)
            sf[h, k, w] = v
        for i in (1, 2, 3):
            to = lax.rem(a4 + i, 4)
            send(sf.at[h, k, to], rf.at[h, k, i - 1], f_s.at[h, k, i - 1], f_r.at[h, k, i - 1], dev(x, y, z + 4 * i, c))

    def finish(h, k):
        t = sf[h, k, a4]
        for i in range(3):
            arrived(rf.at[h, k, i], f_r.at[h, k, i], sib)
            t = t + rf[h, k, i]
        for u in range(4):
            at = h * HALF + k * LANES + u * 256
            out_ref[:, at : at + 256] = t[u * 4 : (u + 1) * 4, :]

    chunks = [(h, k) for k in range(2) for h in range(2)]
    for h, k in chunks:
        if k == 0:
            for j in range(2):
                for i in range(4):
                    arrived(theirs(h, j, i), p_r.at[h, j, 3 + i], sib)
        exchange(h, k, (sel_a, sel_b)[h], (xa, xb)[h])
    for stage in (gathered, fours, finish):
        for h, k in chunks:
            stage(h, k)

    for cp in sent:
        cp.wait_send()


def per_device(tiles, integral_cd_tile, part_dest, partial_row_place, amplitudes, residual_in):
    bf16, f32, i32, dma = jnp.bfloat16, jnp.float32, jnp.int32, pltpu.SemaphoreType.DMA
    hbm = pl.BlockSpec(memory_space=pltpu.HBM)
    ladder = pl.pallas_call(
        ladder_kernel,
        out_shape=jax.ShapeDtypeStruct((4, 4096), f32),
        in_specs=[hbm] * 5,
        out_specs=pl.BlockSpec(memory_space=pltpu.VMEM),
        scratch_shapes=[
            pltpu.SMEM((128,), i32),
            pltpu.VMEM((1, 32), i32),
            pltpu.VMEM((1, 32), i32),
            pltpu.VMEM((4, 4096), bf16),
            pltpu.VMEM((512, 32, 128), bf16),
            pltpu.VMEM((128, 4096), bf16),
            pltpu.VMEM((4096, 128), f32),
            pltpu.VMEM((32, 128, 512), bf16),
            pltpu.VMEM((1024, 128), f32),
            pltpu.VMEM((8, 32, HALF), bf16),
            pltpu.VMEM((8, 32, HALF), bf16),
            pltpu.VMEM((8, 8, 128), i32),
            pltpu.VMEM((8, 8, 128), i32),
            pltpu.VMEM((2, 2, 4, 64, LANES), bf16),
            pltpu.VMEM((2, 2, 3, 64, LANES), bf16),
            pltpu.VMEM((2, 2, 4, 16, LANES), bf16),
            pltpu.VMEM((2, 2, 3, 16, LANES), bf16),
            pltpu.VMEM((2, 2, 4, 16, LANES), f32),
            pltpu.VMEM((2, 2, 4, 16, 256), f32),
            pltpu.VMEM((2, 2, 3, 16, 256), f32),
            dma((5,)),
            dma((2, 16)), dma((2, 16)),
            dma((3,)), dma((3,)),
            dma((5,)), dma((5,)),
            dma((9, 3)), dma((9, 3)),
            dma((5, 4)), dma((5, 4)),
            dma((2, 7)), dma((2, 7)),
            dma((2, 2, 7)), dma((2, 2, 7)),
            dma((2, 2, 3)), dma((2, 2, 3)),
            dma((2, 2, 3)), dma((2, 2, 3)),
            dma((2, 2, 3)), dma((2, 2, 3)),
        ],
        compiler_params=pltpu.CompilerParams(
            collective_id=0, has_side_effects=True, vmem_limit_bytes=63 << 20
        ),
    )(
        integral_cd_tile,
        part_dest.reshape(1, PAB),
        partial_row_place.reshape(1, PAB),
        amplitudes.reshape(4, 4096),
        tiles,
    )
    return residual_in + ladder[None]


def solution(mesh):
    return jax.shard_map(
        per_device,
        mesh=mesh,
        in_specs=(
            P(("rows", "cols"), None),
            P(("rows", "cols")),
            P(("rows", "cols"), None),
            P(("rows", "cols")),
            P("cols", "rows", None),
            P("rows", "cols", None),
        ),
        out_specs=P("rows", "cols", None),
        check_vma=False,
    )
```
